256 devices in a mesh: row: 32 (over z_lo, y, x), col: 8 (over z_hi, core).
Axes of the slice: x: 4, y: 4, z: 8 (z_hi: 4, z_lo: 2; z = z_hi * 2 + z_lo), core: 2. Of those that a mesh axis runs over, the one named last changes fastest.
Arguments:
- positions: float32 [3, 14336], P(None, ('row', 'col')), as said below
- polarizability: float32 [14336], P(('row', 'col')), may hold values from 0.04 to 0.16
- seeds: float32 [3, 16, 14336], P(None, None, ('row', 'col')), may hold values from -6 to 6
- dipoles: float32 [3, 16, 14336], P(None, None, ('row', 'col')), may hold values from -1.8 to 1.8
- tile_mask: int32 [256, 256], P('row', 'col'), may hold values from 0 to 1, as said below
Outputs:
- adjoint_field: float32 [3, 16, 14336], P(None, None, ('row', 'col'))
- gradient: float32 [3, 14336], P(None, ('row', 'col'))
The draws below stay inside these ranges and needn't reach their ends.
Inputs may be any that keep to these rules, and one draw needn't show every extreme that they name: `positions`: beads lie near distinct points of a unit cubic lattice, each coordinate within 0.3 of its point; the points fill a roughly spherical droplet, and the beads of one block are spatially compact clusters of neighbouring points. Read as m_ab = tile_mask[a, (b % 8) * 32 + b // 8], m_ab is 1 exactly when the axis-aligned boxes spanned by the lattice points of blocks a and b lie within a distance of 6 of each other; so the table is symmetric with ones on the diagonal.
All inputs are finite; a program needn't handle non-finite values.
Results may differ from the reference program's by a relative error of at most 0.0003.
Values sent between devices are 32-bit elements; how exact they have to be, the bound alone decides.
No kernel may reach another device: no remote copies, remote signals or barrier semaphores. Data moves between devices by JAX's collectives and lax.ppermute only.
A program may use at most 64 MiB of HBM per device.

```python
import math
import jax
import jax.numpy as jnp
from jax import lax

PROBES = 16
BEAD_DEV = 56
ROW_GROUPS = 32
COL_GROUPS = 8
BLOCKS = 256
BEADS = 14336
CUTOFF = 6


def lattice_side():
    side_len = int(math.ceil((BEADS * 6.0 / math.pi) ** (1.0 / 3.0))) + 2
    return side_len


def droplet_sites(key):
    side_len = lattice_side()
    shift_key, order_key = jax.random.split(jax.random.fold_in(key, 11), 2)
    index_all = jnp.arange(side_len ** 3, dtype=jnp.int32)
    coords = jnp.stack([index_all % side_len, index_all // side_len % side_len, index_all // (side_len * side_len)])
    centred = 2 * coords - (side_len - 1)
    radial = jnp.sum(centred * centred, axis=0)
    chosen = jnp.argsort(radial, stable=True)[:BEADS]
    picked = coords[:, chosen]
    shift = jax.random.randint(shift_key, (3, 1), 0, 8)
    moved = picked + shift
    code = jnp.zeros((BEADS,), jnp.int32)
    for level in range(7):
        for axis_id in range(3):
            bit_value = moved[axis_id] // 2 ** level % 2
            code = code + bit_value * 2 ** (3 * level + axis_id)
    ordered = picked[:, jnp.argsort(code, stable=True)]
    grouped = ordered.reshape(3, BLOCKS, BEAD_DEV)
    block_order = jax.random.permutation(order_key, BLOCKS)
    grouped = grouped[:, block_order, :]
    return grouped


def draw_positions(key, part):
    side_len = lattice_side()
    grouped = droplet_sites(key)
    lattice = grouped.reshape(3, BEADS).astype(jnp.float32)
    jitter_key = jax.random.fold_in(jax.random.fold_in(key, 29), 0)
    jitter = jax.random.uniform(jitter_key, (3, BEADS), jnp.float32, -0.3, 0.3)
    return (lattice + jitter - 0.5 * (side_len - 1)).astype(jnp.float32)


def common_plus_rough(key, label, shown_common, shown_rough):
    common_key = jax.random.fold_in(jax.random.fold_in(key, label), 0)
    rough_key = jax.random.fold_in(jax.random.fold_in(key, label), 2)
    common = jnp.clip(shown_common * jax.random.normal(common_key, (3, PROBES, 1), jnp.float32), -5.0 * shown_common / 3.0, 5.0 * shown_common / 3.0)
    rough = jnp.clip(shown_rough * jax.random.normal(rough_key, (3, PROBES, BEADS), jnp.float32), -3.0 * shown_rough, 3.0 * shown_rough)
    return (common + rough).astype(jnp.float32)


def draw_seeds(key, part):
    return common_plus_rough(key, 41, 1.5, 1.0)


def draw_dipoles(key, part):
    return common_plus_rough(key, 53, 0.48, 0.3)


def draw_tile_mask(key, part):
    grouped = droplet_sites(key)
    lowest = jnp.min(grouped, axis=2)
    highest = jnp.max(grouped, axis=2)
    gap_one = lowest[:, None, :] - highest[:, :, None]
    gap_two = lowest[:, :, None] - highest[:, None, :]
    gap = jnp.maximum(jnp.maximum(gap_one, gap_two), 0)
    gap_sq = jnp.sum(gap * gap, axis=0)
    full_table = (gap_sq <= CUTOFF * CUTOFF).astype(jnp.int32)
    return full_table.reshape(BLOCKS, ROW_GROUPS, COL_GROUPS).transpose(0, 2, 1).reshape(BLOCKS, BLOCKS).astype(jnp.int32)


def block_levels(own_key, shape, cuts, low, largest):
    factor_of, own = 1.0, jax.random.fold_in(own_key, 6)
    for axis_at, parts in cuts:
        heights = jnp.exp(jax.random.uniform(jax.random.fold_in(own, axis_at), (parts,), jnp.float32, low / len(cuts), largest / len(cuts)))
        factor_of = factor_of * jnp.repeat(heights, shape[axis_at] // parts).reshape([-1 if axis == axis_at else 1 for axis in range(len(shape))])
    return factor_of


def setup_inputs(seed: int = 0) -> dict:
    streams_of = jax.random.split(jax.random.key(seed), 6)
    return {
        "positions": draw_positions(jax.random.fold_in(streams_of[5], 71), 0),
        "polarizability": jnp.clip(jnp.exp(math.log(0.16) - 1.3862944 * jax.random.uniform(streams_of[1], (BEADS,), jnp.float32) ** block_levels(streams_of[1], (BEADS,), ((0, 256),), -0.2, 0.2)), 0.04, 0.16),
        "seeds": draw_seeds(jax.random.fold_in(streams_of[5], 71), 0),
        "dipoles": draw_dipoles(jax.random.fold_in(streams_of[5], 71), 0),
        "tile_mask": draw_tile_mask(jax.random.fold_in(streams_of[5], 71), 0),
    }


THOLE_DAMPING = 0.39
HIGHEST = lax.Precision.HIGHEST

def pair_terms(row_geom, col_geom, keep_mask):
    offset = row_geom[:3, :, None] - col_geom[:3, None, :]
    dist_sq = lax.optimization_barrier(jnp.sum(offset * offset, axis=0))
    dist_sq = jnp.where(keep_mask > 0.0, dist_sq, 1.0)
    inverse = lax.rsqrt(dist_sq)
    damping = THOLE_DAMPING * dist_sq * (dist_sq * inverse) * row_geom[3][:, None] * col_geom[3][None, :]
    damp_exp = jnp.exp(-damping)
    inv_cube = keep_mask * inverse * inverse * inverse
    isotropic = (1.0 - damp_exp) * inv_cube
    radial = 3.0 * (1.0 - (1.0 + damping) * damp_exp) * inv_cube * inverse * inverse
    tensor = radial[None, None] * offset[:, None] * offset[None, :]
    return (tensor, isotropic)

def apply_rows(tensor, isotropic, vector):
    result = jnp.einsum('abij,bpj->api', tensor, vector, precision=HIGHEST)
    return result - jnp.einsum('ij,apj->api', isotropic, vector, precision=HIGHEST)

def reference(positions, polarizability, seeds, dipoles, tile_mask):
    bead_count = positions.shape[1]
    block_size = BEAD_DEV
    blocks = bead_count // block_size
    probes = seeds.shape[1]
    block_mask = tile_mask.reshape(blocks, COL_GROUPS, ROW_GROUPS).transpose(0, 2, 1).reshape(blocks, blocks)
    block_mask = block_mask.astype(positions.dtype)
    geometry = jnp.concatenate([positions, lax.rsqrt(polarizability)[None, :]], axis=0)
    column_ids = jnp.arange(bead_count, dtype=jnp.int32)
    geom_split = geometry.reshape(4, blocks, block_size).transpose(1, 0, 2)
    offsets = jnp.arange(blocks, dtype=jnp.int32)

    def keep_for(index, row_mask):
        row_ids = index * block_size + jnp.arange(block_size, dtype=jnp.int32)
        spread = jnp.repeat(row_mask, block_size)
        return spread[None, :] * (row_ids[:, None] != column_ids[None, :]).astype(positions.dtype)

    def sweep_field(vector):

        def one_block(inputs):
            index, geom_rows, row_mask = inputs
            tensor, isotropic = pair_terms(geom_rows, geometry, keep_for(index, row_mask))
            return apply_rows(tensor, isotropic, vector)
        blockwise = lax.map(one_block, (offsets, geom_split, block_mask))
        return jnp.moveaxis(blockwise, 0, -2).reshape(3, probes, bead_count)
    field_one = seeds + sweep_field(polarizability[None, None, :] * seeds)
    field_two = seeds + sweep_field(polarizability[None, None, :] * field_one)
    adjoint = polarizability[None, None, :] * field_two
    adjoint_split = jnp.moveaxis(adjoint.reshape(3, probes, blocks, block_size), 2, 0)

    def pair_score(geom_rows, geom_all, keep_mask, adjoint_rows):
        tensor, isotropic = pair_terms(geom_rows, geom_all, keep_mask)
        return jnp.sum(adjoint_rows * apply_rows(tensor, isotropic, dipoles))
    slopes = jax.grad(pair_score, argnums=(0, 1))

    def force_step(running, inputs):
        index, geom_rows, row_mask, adjoint_rows = inputs
        slope_rows, slope_all = slopes(geom_rows, geometry, keep_for(index, row_mask), adjoint_rows)
        return (running + slope_all[:3], slope_rows[:3])
    start_sum = jnp.zeros((3, bead_count), positions.dtype)
    running, row_slopes = lax.scan(force_step, start_sum, (offsets, geom_split, block_mask, adjoint_split))
    gradient = running + jnp.moveaxis(row_slopes, 0, 1).reshape(3, bead_count)
    return (field_two, gradient)
```

```python
import jax
import jax.numpy as jnp
from jax import lax
from jax.experimental import pallas as pl
from jax.experimental.pallas import tpu as pltpu
from jax.sharding import PartitionSpec as P

THOLE_DAMPING = 0.39
HIGHEST = lax.Precision.HIGHEST
F32 = jnp.float32
BF16 = jnp.bfloat16

BEAD = 56
NROW = 32
NCOL = 8
RB = NCOL * BEAD
CB = NROW * BEAD
LANE = 128
PAIRS = ((0, 0), (1, 1), (2, 2), (0, 1), (0, 2), (1, 2))
VMEM_SPEC = pl.BlockSpec(memory_space=pltpu.VMEM)


def dot_f32(a, b, dims, precision=None):
    return lax.dot_general(a, b, (dims, ((), ())), precision=precision, preferred_element_type=F32)


def hi_lo(x):
    hi = x.astype(BF16).astype(F32)
    return hi, x - hi


def lane_ids(shape):
    return lax.broadcasted_iota(jnp.int32, shape, 1)


def arranged(u, a, b):
    group = (lane_ids(u.shape) % 64) // 16
    if a == b:
        return jnp.where(group == a, u, 0.0)
    step = 16 * (b - a)
    down = pltpu.roll(u, LANE - step, 1)
    up = pltpu.roll(u, step, 1)
    return jnp.where(group == a, down, jnp.where(group == b, up, 0.0))


def build_kernel(gc_ref, gr_ref, mask_ref, t_ref, f5_ref, g7_ref, xc_ref, y_ref, w_ref, m_ref):
    for k in range(CB // 256):
        rows = pl.ds(k * 256, 256)
        g = gc_ref[rows, :]
        pick = (lane_ids((8, LANE)) == 96 + lax.broadcasted_iota(jnp.int32, (8, LANE), 0)).astype(F32)
        xc_ref[:, rows] = dot_f32(pick, g, ((1,), (1,)), HIGHEST)
        v = jnp.where(lane_ids(g.shape) < 48, g, 0.0)
        hi, lo = hi_lo(v)
        u = hi + pltpu.roll(lo, 64, 1)
        for n, (a, b) in enumerate(PAIRS):
            w_ref[n, rows, :] = arranged(u, a, b).astype(BF16)
    block = lax.broadcasted_iota(jnp.int32, (NROW, CB), 1) // BEAD
    owner = lax.broadcasted_iota(jnp.int32, (NROW, CB), 0)
    chosen = (block == owner).astype(BF16)
    keep_all = dot_f32(mask_ref[...].astype(F32).astype(BF16), chosen, ((1,), (0,)))
    for k in range(NCOL):
        m_ref[k] = jnp.broadcast_to(keep_all[k : k + 1], (8, CB))

    def row_chunk(q, carry):
        r0 = pl.multiple_of(q * 16, 16)
        rows = pl.ds(r0, 16)
        g = gr_ref[rows, :]
        xr, yr, zr, sr = (jnp.broadcast_to(g[:, 96 + k : 97 + k], (16, LANE)) for k in range(4))
        sr = sr * THOLE_DAMPING
        first = (2 * q) // 7
        second = (2 * q + 1) // 7
        for k in range(CB // LANE):
            cols = pl.ds(k * LANE, LANE)
            row_of = lambda i: jnp.broadcast_to(xc_ref[i : i + 1, cols], (16, LANE))
            keep = jnp.concatenate(
                [
                    m_ref[first, :, cols],
                    m_ref[second, :, cols],
                ],
                axis=0,
            )
            dx, dy, dz = xr - row_of(0), yr - row_of(1), zr - row_of(2)
            r2 = dx * dx + dy * dy + dz * dz
            inv = lax.rsqrt(jnp.maximum(r2, 1e-12)) * keep
            v = (r2 * (r2 * inv)) * (sr * row_of(3))
            e = jnp.exp(-v)
            ve = v * e
            one = 1.0 - e
            inv2 = inv * inv
            inv3 = inv2 * inv
            f3 = one * inv3
            inv5 = inv3 * inv2
            f5 = ((one - ve) * 3.0) * inv5
            g7 = inv2 * ((v * ve) * inv5 * 9.0 - 5.0 * f5)
            f5_ref[rows, cols] = f5
            g7_ref[rows, cols] = g7
            fx, fy, fz = f5 * dx, f5 * dy, f5 * dz
            parts = (fx * dx - f3, fy * dy - f3, fz * dz - f3, fx * dy, fx * dz, fy * dz)
            for n, t in enumerate(parts):
                hi = t.astype(BF16)
                t_ref[n, rows, cols] = hi
                t_ref[6 + n, rows, cols] = (t - hi.astype(F32)).astype(BF16)
        return carry

    lax.fori_loop(0, RB // 16, row_chunk, 0)
    for q in range(4):
        rows = pl.ds(q * 112, 112)
        total = jnp.zeros((112, LANE), F32)
        for n in range(12):
            total += dot_f32(t_ref[n, rows, :], w_ref[n % 6], ((1,), (0,)))
        y = total + pltpu.roll(total, 64, 1)
        y_ref[rows, :] = y


def second_kernel(got_ref, gr_ref, t_ref, out_ref, w_ref, y_ref):
    y = got_ref[0]
    for k in range(1, NCOL):
        y = y + got_ref[k]
    y = jnp.concatenate([y, pltpu.roll(y, 64, 1)], axis=0)
    g = gr_ref[...]
    lanes = lane_ids((RB, LANE))
    pol = jnp.broadcast_to(g[:, 100:101], (RB, LANE))
    vec = jnp.where(lanes < 48, g + pol * y, 0.0)
    hi, lo = hi_lo(vec)
    u = hi + pltpu.roll(lo, 64, 1)
    ut = u.T
    group = (lax.broadcasted_iota(jnp.int32, (LANE, RB), 0) % 64) // 16
    for n, (a, b) in enumerate(PAIRS):
        if a == b:
            w = jnp.where(group == a, ut, 0.0)
        else:
            step = 16 * (b - a)
            down = jnp.concatenate([ut[step:], ut[:step]], axis=0)
            up = jnp.concatenate([ut[LANE - step :], ut[: LANE - step]], axis=0)
            w = jnp.where(group == a, down, jnp.where(group == b, up, 0.0))
        w_ref[n] = w.astype(BF16)
    for k in range(7):
        cols = pl.ds(k * 256, 256)
        total = jnp.zeros((LANE, 256), F32)
        for n in range(12):
            total += dot_f32(w_ref[n % 6], t_ref[n, :, cols], ((1,), (0,)))
        y_ref[:, cols] = total[0:48] + total[64:112]
    for j in range(NROW):
        out_ref[j, :, 0:BEAD] = y_ref[0:24, j * BEAD : (j + 1) * BEAD]
        out_ref[j, :, 64 : 64 + BEAD] = y_ref[24:48, j * BEAD : (j + 1) * BEAD]


def own_kernel(got_ref, seeds_ref, pol_ref, field_ref, next_ref):
    y = got_ref[0]
    for k in range(1, NROW):
        y = y + got_ref[k]
    y = jnp.concatenate([y, pltpu.roll(y, 64, 1)], axis=0)
    field = seeds_ref[...] + y[:, 0:BEAD]
    field_ref[...] = field
    vec = pol_ref[...] * field
    pad = jnp.concatenate([vec, jnp.zeros((48, LANE - BEAD), F32)], axis=1)
    pad = jnp.concatenate([pad, jnp.zeros((LANE - 48, LANE), F32)], axis=0)
    turned = pad.T
    next_ref[...] = turned[0:BEAD]


def gradient_kernel(
    a_ref, gc_ref, gr_ref, f5_ref, g7_ref, xc_ref, or_ref, oc_ref, l_ref, m_ref, h_ref, racc_ref, cacc_ref
):
    a = a_ref[...]
    ahi, alo = hi_lo(a)
    ahi = ahi + pltpu.roll(ahi, 64, 1)
    alo = alo + pltpu.roll(alo, 64, 1)
    for n, (p, q) in enumerate(PAIRS):
        scale = 2.0 if p == q else 1.0
        l_ref[n, :, 0:LANE] = (arranged(ahi, p, q) * scale).astype(BF16)
        l_ref[n, :, LANE:] = (arranged(alo, p, q) * scale).astype(BF16)
    for k in range(CB // 256):
        rows = pl.ds(k * 256, 256)
        g = gc_ref[rows, :]
        mu = jnp.where(lane_ids(g.shape) < 48, pltpu.roll(g, 80, 1), 0.0)
        hi, lo = hi_lo(mu)
        u = (hi + pltpu.roll(lo, 64, 1)).astype(BF16)
        m_ref[rows, 0:LANE] = u
        m_ref[rows, LANE:] = u
    racc_ref[...] = jnp.zeros_like(racc_ref)

    def col_chunk(k, carry):
        c0 = pl.multiple_of(k * 256, 256)
        cols = pl.ds(c0, 256)
        for n in range(6):
            h_ref[n] = dot_f32(l_ref[n], m_ref[cols, :], ((1,), (1,)))
        xc, yc, zc = (jnp.broadcast_to(xc_ref[i : i + 1, cols], (8, 256)) for i in range(3))

        def rows_step(t, acc):
            r0 = pl.multiple_of(t * 8, 8)
            rows = pl.ds(r0, 8)
            g = gr_ref[rows, :]
            xr, yr, zr = (jnp.broadcast_to(g[:, 96 + i : 97 + i], (8, 256)) for i in range(3))
            dx, dy, dz = xr - xc, yr - yc, zr - zc
            hxx, hyy, hzz, hxy, hxz, hyz = (h_ref[n, rows, :] for n in range(6))
            wx = hxx * dx + hxy * dy + hxz * dz
            wy = hxy * dx + hyy * dy + hyz * dz
            wz = hxz * dx + hyz * dy + hzz * dz
            f5 = f5_ref[rows, cols]
            e = g7_ref[rows, cols] * (wx * dx + wy * dy + wz * dz) + f5 * (hxx + hyy + hzz)
            f52 = f5 + f5
            out = []
            for i, (d, w) in enumerate(((dx, wx), (dy, wy), (dz, wz))):
                s = e * d + f52 * w
                racc_ref[i, rows, :] += s[:, 0:LANE] + s[:, LANE:]
                out.append(acc[i] + s)
            return tuple(out)

        zero = jnp.zeros((8, 256), F32)
        acc = lax.fori_loop(0, RB // 8, rows_step, (zero, zero, zero), unroll=2)
        for i in range(3):
            cacc_ref[i : i + 1, cols] = -0.5 * jnp.sum(acc[i], axis=0, keepdims=True)
        return carry

    lax.fori_loop(0, CB // 256, col_chunk, 0)
    ones = jnp.full((8, LANE), 0.5, F32)
    row = lax.broadcasted_iota(jnp.int32, (8, RB), 0)
    total = jnp.zeros((8, RB), F32)
    for i in range(3):
        part = dot_f32(ones, racc_ref[i], ((1,), (1,)), HIGHEST)
        total = jnp.where(row == i, part, total)
    racc_ref[0, 0:8, :] = total[:, 0:LANE]
    racc_ref[0, 8:16, :] = total[:, LANE : 2 * LANE]
    for j in range(NCOL):
        or_ref[j, :, 0:BEAD] = total[:, j * BEAD : (j + 1) * BEAD]
    for j in range(NROW):
        oc_ref[j, :, 0:BEAD] = cacc_ref[:, j * BEAD : (j + 1) * BEAD]


def final_kernel(rgot_ref, cgot_ref, out_ref):
    total = rgot_ref[0]
    for k in range(1, NCOL):
        total = total + rgot_ref[k]
    for k in range(NROW):
        total = total + cgot_ref[k]
    out_ref[...] = total[0:3, 0:BEAD]


def call(kernel, outs, scratch, flops, limit_mib):
    return pl.pallas_call(
        kernel,
        out_shape=[jax.ShapeDtypeStruct(s, t) for s, t in outs],
        out_specs=[VMEM_SPEC] * len(outs),
        scratch_shapes=[pltpu.VMEM(s, t) for s, t in scratch],
        compiler_params=pltpu.CompilerParams(vmem_limit_bytes=limit_mib << 20),
        cost_estimate=pl.CostEstimate(flops=flops, bytes_accessed=4_000_000, transcendentals=0),
    )


def run_build(gc, gr, mask):
    return call(
        build_kernel,
        [((12, RB, CB), BF16), ((RB, CB), F32), ((RB, CB), F32), ((8, CB), F32), ((RB, LANE), F32)],
        [((6, CB, LANE), BF16), ((NCOL, 8, CB), F32)],
        400_000_000,
        12,
    )(gc, gr, mask)


def run_second(got, gr, t):
    return call(
        second_kernel,
        [((NROW, 24, LANE), F32)],
        [((6, LANE, RB), BF16), ((48, CB), F32)],
        200_000_000,
        12,
    )(got, gr, t)[0]


def run_own(got, seeds, pol):
    return call(own_kernel, [((48, BEAD), F32), ((BEAD, LANE), F32)], [], 100_000, 4)(got, seeds, pol)


def run_gradient(a, gc, gr, f5, g7, xc):
    return call(
        gradient_kernel,
        [((NCOL, 8, LANE), F32), ((NROW, 8, LANE), F32)],
        [
            ((6, RB, 2 * LANE), BF16),
            ((CB, 2 * LANE), BF16),
            ((6, RB, 256), F32),
            ((3, RB, LANE), F32),
            ((8, CB), F32),
        ],
        300_000_000,
        12,
    )(a, gc, gr, f5, g7, xc)


def broadcast_all(x, axis):
    n = lax.axis_size(axis)
    return lax.all_to_all(jnp.broadcast_to(x[None], (n, *x.shape)), axis, 0, 0, tiled=True)


def exchange(x, axis):
    return lax.all_to_all(x, axis, 0, 0, tiled=True)


def local(positions, polarizability, seeds, dipoles, tile_mask):
    seeds = seeds.reshape(48, BEAD)
    dipoles = dipoles.reshape(48, BEAD)
    pol = polarizability[None, :]
    own = jnp.concatenate(
        [pol * seeds, dipoles, positions, lax.rsqrt(pol), pol, jnp.zeros((27, BEAD), F32)], axis=0
    ).T
    gc = broadcast_all(own, "row").reshape(CB, LANE)
    gr = broadcast_all(own, "col").reshape(RB, LANE)
    t, f5, g7, xc, y1 = run_build(gc, gr, tile_mask)
    half = jnp.concatenate([y1[: RB // 2, 0:64], y1[RB // 2 :, 0:64]], axis=1)
    got = broadcast_all(half, "col")
    got2 = exchange(run_second(got, gr, t), "row")
    field, nxt = run_own(got2, seeds, pol)
    a = broadcast_all(nxt, "col").reshape(RB, LANE)
    out_r, out_c = run_gradient(a, gc, gr, f5, g7, xc)
    rgot = exchange(out_r, "col")
    cgot = exchange(out_c, "row")
    (gradient,) = call(final_kernel, [((3, BEAD), F32)], [], 100_000, 4)(rgot, cgot)
    return (field.reshape(3, 16, BEAD), gradient)


def solution(mesh):
    in_specs = (
        P(None, ("row", "col")),
        P(("row", "col")),
        P(None, None, ("row", "col")),
        P(None, None, ("row", "col")),
        P("row", "col"),
    )
    out_specs = (P(None, None, ("row", "col")), P(None, ("row", "col")))
    return jax.shard_map(local, mesh=mesh, in_specs=in_specs, out_specs=out_specs, check_vma=False)
```

```python
import jax
import jax.numpy as jnp
from jax import lax
from jax.experimental import pallas as pl
from jax.experimental.pallas import tpu as pltpu
from jax.sharding import PartitionSpec as P

THOLE_DAMPING = 0.39
HIGHEST = lax.Precision.HIGHEST
F32 = jnp.float32
BF16 = jnp.bfloat16

BEAD = 56
NROW = 32
NCOL = 8
RB = NCOL * BEAD
CB = NROW * BEAD
LANE = 128
GEO = 48
PAIRS = ((0, 0), (1, 1), (2, 2), (0, 1), (0, 2), (1, 2))
VMEM_SPEC = pl.BlockSpec(memory_space=pltpu.VMEM)


def dot_f32(a, b, dims, precision=None):
    return lax.dot_general(a, b, (dims, ((), ())), precision=precision, preferred_element_type=F32)


def hi_lo(x):
    hi = x.astype(BF16).astype(F32)
    return hi, x - hi


def lane_ids(shape):
    return lax.broadcasted_iota(jnp.int32, shape, 1)


def vector_lanes(x):
    return jnp.where(lane_ids(x.shape) < GEO, x, 0.0)


def arranged(u, a, b):
    group = (lane_ids(u.shape) % 64) // 16
    if a == b:
        return jnp.where(group == a, u, 0.0)
    step = 16 * (b - a)
    down = pltpu.roll(u, LANE - step, 1)
    up = pltpu.roll(u, step, 1)
    return jnp.where(group == a, down, jnp.where(group == b, up, 0.0))


def unpack(got_ref, out_ref, blocks):
    for j in range(blocks):
        piece = got_ref[j]
        out_ref[j * BEAD : j * BEAD + 32, :] = piece
        out_ref[j * BEAD + 32 : (j + 1) * BEAD, :] = pltpu.roll(piece[0:24], 64, 1)


def prep_kernel(seeds_ref, dip_ref, pos_ref, pol_ref, v_ref, mu_ref):
    pol = pol_ref[...]
    row = lax.broadcasted_iota(jnp.int32, (16, BEAD), 0)
    geo = jnp.where(row == 3, lax.rsqrt(pol), jnp.where(row == 4, pol, 0.0))
    for i in range(3):
        geo = jnp.where(row == i, pos_ref[i : i + 1, :], geo)
    both = jnp.concatenate([pol * seeds_ref[...], geo, dip_ref[...], geo], axis=0)
    both = jnp.concatenate([both, jnp.zeros((LANE, LANE - BEAD), F32)], axis=1)
    turned = both.T
    swapped = pltpu.roll(turned, 64, 1)
    left = lane_ids((32, LANE)) < 64
    v_ref[...] = jnp.where(left, turned[0:32], swapped[32:64])
    mu_ref[...] = jnp.where(left, swapped[0:32], turned[32:64])


def column_kernel(got_ref, mask_ref, w_ref, xc_ref, m_ref, g_ref):
    unpack(got_ref, g_ref, NROW)
    pick = (lane_ids((8, LANE)) == GEO + lax.broadcasted_iota(jnp.int32, (8, LANE), 0)).astype(F32)
    for k in range(CB // 256):
        rows = pl.ds(k * 256, 256)
        g = g_ref[rows, :]
        xc_ref[:, rows] = dot_f32(pick, g, ((1,), (1,)), HIGHEST)
        hi, lo = hi_lo(vector_lanes(g))
        u = hi + pltpu.roll(lo, 64, 1)
        for n, (a, b) in enumerate(PAIRS):
            w_ref[n, rows, :] = arranged(u, a, b).astype(BF16)
    block = lax.broadcasted_iota(jnp.int32, (NROW, CB), 1) // BEAD
    owner = lax.broadcasted_iota(jnp.int32, (NROW, CB), 0)
    chosen = (block == owner).astype(BF16)
    keep_all = dot_f32(mask_ref[...].astype(F32).astype(BF16), chosen, ((1,), (0,)))
    for k in range(NCOL):
        m_ref[k] = jnp.broadcast_to(keep_all[k : k + 1], (8, CB))


def moment_kernel(got_ref, l_ref, g_ref):
    unpack(got_ref, g_ref, NCOL)
    hi, lo = hi_lo(vector_lanes(g_ref[...]))
    hi = hi + pltpu.roll(hi, 64, 1)
    lo = lo + pltpu.roll(lo, 64, 1)
    for n, (p, q) in enumerate(PAIRS):
        scale = 2.0 if p == q else 1.0
        l_ref[n, :, 0:LANE] = (arranged(hi, p, q) * scale).astype(BF16)
        l_ref[n, :, LANE:] = (arranged(lo, p, q) * scale).astype(BF16)


def build_kernel(
    got_ref, w_ref, xc_ref, m_ref, t_ref, f5_ref, g7_ref, xb_ref, out_ref, g_ref, y_ref
):
    unpack(got_ref, g_ref, NCOL)
    for i in range(4):
        spread = jnp.broadcast_to(g_ref[:, GEO + i : GEO + i + 1], (RB, LANE))
        xb_ref[i] = spread * THOLE_DAMPING if i == 3 else spread

    def row_chunk(q, carry):
        r0 = pl.multiple_of(q * 16, 16)
        rows = pl.ds(r0, 16)
        xr, yr, zr, sr = (xb_ref[i, rows, :] for i in range(4))
        first = (2 * q) // 7
        second = (2 * q + 1) // 7
        for k in range(CB // LANE):
            cols = pl.ds(k * LANE, LANE)
            xc, yc, zc, sc = (jnp.broadcast_to(xc_ref[i : i + 1, cols], (16, LANE)) for i in range(4))
            keep = jnp.concatenate([m_ref[first, :, cols], m_ref[second, :, cols]], axis=0)
            dx, dy, dz = xr - xc, yr - yc, zr - zc
            r2 = dx * dx + dy * dy + dz * dz
            inv = lax.rsqrt(jnp.maximum(r2, 1e-12)) * keep
            v = (r2 * (r2 * inv)) * (sr * sc)
            e = jnp.exp(-v)
            ve = v * e
            one = 1.0 - e
            inv2 = inv * inv
            inv3 = inv2 * inv
            f3 = one * inv3
            inv5 = inv3 * inv2
            f5 = ((one - ve) * 3.0) * inv5
            g7 = inv2 * ((v * ve) * inv5 * 9.0 - 5.0 * f5)
            f5_ref[rows, cols] = f5
            g7_ref[rows, cols] = g7
            fx, fy, fz = f5 * dx, f5 * dy, f5 * dz
            parts = (fx * dx - f3, fy * dy - f3, fz * dz - f3, fx * dy, fx * dz, fy * dz)
            for n, t in enumerate(parts):
                hi = t.astype(BF16)
                t_ref[n, rows, cols] = hi
                t_ref[6 + n, rows, cols] = (t - hi.astype(F32)).astype(BF16)
        return carry

    lax.fori_loop(0, RB // 16, row_chunk, 0)
    total = dot_f32(t_ref[0], w_ref[0], ((1,), (0,)))
    for n in range(1, 12):
        total += dot_f32(t_ref[n], w_ref[n % 6], ((1,), (0,)))
    y_ref[...] = total + pltpu.roll(total, 64, 1)
    left = lane_ids((24, LANE)) < 64
    for k in range(NCOL):
        at = k * BEAD
        out_ref[k, 0:24, :] = jnp.where(left, y_ref[at : at + 24, :], y_ref[at + 32 : at + 56, :])
        out_ref[k, 24:32, :] = y_ref[at + 24 : at + 32, :]


def first_own_kernel(got_ref, v_ref, out_ref):
    y = got_ref[0]
    for k in range(1, NCOL):
        y = y + got_ref[k]
    v = v_ref[...]
    lanes = lane_ids((32, LANE))
    pol = jnp.where(
        lanes < 64,
        jnp.broadcast_to(v[:, GEO + 4 : GEO + 5], (32, LANE)),
        jnp.broadcast_to(v[:, 64 + GEO + 4 : 64 + GEO + 5], (32, LANE)),
    )
    out_ref[...] = jnp.where(lanes % 64 < GEO, v + pol * y, 0.0)


def second_kernel(got_ref, t_ref, out_ref, g_ref, w_ref, y_ref):
    unpack(got_ref, g_ref, NCOL)
    hi, lo = hi_lo(vector_lanes(g_ref[...]))
    ut = (hi + pltpu.roll(lo, 64, 1)).T
    group = (lax.broadcasted_iota(jnp.int32, (LANE, RB), 0) % 64) // 16
    for n, (a, b) in enumerate(PAIRS):
        if a == b:
            w = jnp.where(group == a, ut, 0.0)
        else:
            step = 16 * (b - a)
            down = jnp.concatenate([ut[step:], ut[:step]], axis=0)
            up = jnp.concatenate([ut[LANE - step :], ut[: LANE - step]], axis=0)
            w = jnp.where(group == a, down, jnp.where(group == b, up, 0.0))
        w_ref[n] = w.astype(BF16)
    for k in range(7):
        cols = pl.ds(k * 256, 256)
        total = jnp.zeros((LANE, 256), F32)
        for n in range(12):
            total += dot_f32(w_ref[n % 6], t_ref[n, :, cols], ((1,), (0,)))
        y_ref[:, cols] = total[0:48] + total[64:112]
    for j in range(NROW):
        out_ref[j, :, 0:BEAD] = y_ref[0:24, j * BEAD : (j + 1) * BEAD]
        out_ref[j, :, 64 : 64 + BEAD] = y_ref[24:48, j * BEAD : (j + 1) * BEAD]


def second_own_kernel(got_ref, seeds_ref, pol_ref, field_ref, next_ref):
    y = got_ref[0]
    for k in range(1, NROW):
        y = y + got_ref[k]
    y = jnp.concatenate([y, pltpu.roll(y, 64, 1)], axis=0)
    field = seeds_ref[...] + y[:, 0:BEAD]
    field_ref[...] = field
    vec = pol_ref[...] * field
    vec = jnp.concatenate([vec, jnp.zeros((48, LANE - BEAD), F32)], axis=1)
    turned = jnp.concatenate([vec, jnp.zeros((LANE - 48, LANE), F32)], axis=0).T
    left = lane_ids((32, LANE)) < 64
    next_ref[...] = jnp.where(left, turned[0:32], pltpu.roll(turned[32:64], 64, 1))


def gradient_kernel(
    got_ref, l_ref, xb_ref, f5_ref, g7_ref, xc_ref, or_ref, oc_ref, g_ref, m_ref, h_ref, racc_ref, cacc_ref
):
    unpack(got_ref, g_ref, NROW)
    for k in range(CB // 256):
        rows = pl.ds(k * 256, 256)
        hi, lo = hi_lo(vector_lanes(g_ref[rows, :]))
        u = (hi + pltpu.roll(lo, 64, 1)).astype(BF16)
        m_ref[rows, 0:LANE] = u
        m_ref[rows, LANE:] = u
    racc_ref[...] = jnp.zeros_like(racc_ref)

    def col_chunk(k, carry):
        c0 = pl.multiple_of(k * 256, 256)
        cols = pl.ds(c0, 256)
        for n in range(6):
            h_ref[n] = dot_f32(l_ref[n], m_ref[cols, :], ((1,), (1,)))
        xc, yc, zc = (jnp.broadcast_to(xc_ref[i : i + 1, cols], (8, 256)) for i in range(3))

        def rows_step(t, acc):
            r0 = pl.multiple_of(t * 8, 8)
            rows = pl.ds(r0, 8)
            xr, yr, zr = (jnp.concatenate([xb_ref[i, rows, :]] * 2, axis=1) for i in range(3))
            dx, dy, dz = xr - xc, yr - yc, zr - zc
            hxx, hyy, hzz, hxy, hxz, hyz = (h_ref[n, rows, :] for n in range(6))
            wx = hxx * dx + hxy * dy + hxz * dz
            wy = hxy * dx + hyy * dy + hyz * dz
            wz = hxz * dx + hyz * dy + hzz * dz
            f5 = f5_ref[rows, cols]
            e = g7_ref[rows, cols] * (wx * dx + wy * dy + wz * dz) + f5 * (hxx + hyy + hzz)
            f52 = f5 + f5
            out = []
            for i, (d, w) in enumerate(((dx, wx), (dy, wy), (dz, wz))):
                s = e * d + f52 * w
                racc_ref[i, rows, :] += s[:, 0:LANE] + s[:, LANE:]
                out.append(acc[i] + s)
            return tuple(out)

        zero = jnp.zeros((8, 256), F32)
        acc = lax.fori_loop(0, RB // 8, rows_step, (zero, zero, zero), unroll=4)
        for i in range(3):
            cacc_ref[i : i + 1, cols] = -0.5 * jnp.sum(acc[i], axis=0, keepdims=True)
        return carry

    lax.fori_loop(0, CB // 256, col_chunk, 0)
    ones = jnp.full((8, LANE), 0.5, F32)
    row = lax.broadcasted_iota(jnp.int32, (8, RB), 0)
    total = jnp.zeros((8, RB), F32)
    for i in range(3):
        part = dot_f32(ones, racc_ref[i], ((1,), (1,)), HIGHEST)
        total = jnp.where(row == i, part, total)
    for j in range(NCOL):
        or_ref[j, :, 0:BEAD] = total[:, j * BEAD : (j + 1) * BEAD]
    for j in range(NROW):
        oc_ref[j, :, 0:BEAD] = cacc_ref[:, j * BEAD : (j + 1) * BEAD]


def final_kernel(rgot_ref, cgot_ref, out_ref):
    total = rgot_ref[0]
    for k in range(1, NCOL):
        total = total + rgot_ref[k]
    for k in range(NROW):
        total = total + cgot_ref[k]
    out_ref[...] = total[0:3, 0:BEAD]


def call(kernel, outs, scratch, flops, limit_mib):
    return pl.pallas_call(
        kernel,
        out_shape=[jax.ShapeDtypeStruct(s, t) for s, t in outs],
        out_specs=[VMEM_SPEC] * len(outs),
        scratch_shapes=[pltpu.VMEM(s, t) for s, t in scratch],
        compiler_params=pltpu.CompilerParams(vmem_limit_bytes=limit_mib << 20),
        cost_estimate=pl.CostEstimate(flops=flops, bytes_accessed=1_000_000, transcendentals=0),
    )


def run_prep(seeds, dipoles, positions, pol):
    outs = [((32, LANE), F32)] * 2
    return call(prep_kernel, outs, [], 100_000, 4)(seeds, dipoles, positions, pol)


def run_columns(got, mask):
    outs = [((6, CB, LANE), BF16), ((8, CB), F32), ((NCOL, 8, CB), F32)]
    return call(column_kernel, outs, [((CB, LANE), F32)], 2_000_000, 8)(got, mask)


def run_moments(got):
    return call(moment_kernel, [((6, RB, 2 * LANE), BF16)], [((RB, LANE), F32)], 1_000_000, 4)(got)[0]


def run_build(got, w, xc, m):
    outs = [
        ((12, RB, CB), BF16),
        ((RB, CB), F32),
        ((RB, CB), F32),
        ((4, RB, LANE), F32),
        ((NCOL, 32, LANE), F32),
    ]
    scratch = [((RB, LANE), F32), ((RB, LANE), F32)]
    return call(build_kernel, outs, scratch, 400_000_000, 6)(got, w, xc, m)


def run_first_own(got, v):
    return call(first_own_kernel, [((32, LANE), F32)], [], 100_000, 4)(got, v)[0]


def run_second(got, t):
    scratch = [((RB, LANE), F32), ((6, LANE, RB), BF16), ((48, CB), F32)]
    return call(second_kernel, [((NROW, 24, LANE), F32)], scratch, 200_000_000, 6)(got, t)[0]


def run_second_own(got, seeds, pol):
    outs = [((48, BEAD), F32), ((32, LANE), F32)]
    return call(second_own_kernel, outs, [], 100_000, 4)(got, seeds, pol)


def run_gradient(got, l, xb, f5, g7, xc):
    outs = [((NCOL, 8, LANE), F32), ((NROW, 8, LANE), F32)]
    scratch = [
        ((CB, LANE), F32),
        ((CB, 2 * LANE), BF16),
        ((6, RB, 256), F32),
        ((3, RB, LANE), F32),
        ((8, CB), F32),
    ]
    return call(gradient_kernel, outs, scratch, 300_000_000, 10)(got, l, xb, f5, g7, xc)


def run_final(rgot, cgot):
    return call(final_kernel, [((3, BEAD), F32)], [], 100_000, 4)(rgot, cgot)[0]


def exchange(x, axis):
    return lax.all_to_all(x, axis, 0, 0, tiled=True)


def broadcast_all(x, axis):
    return exchange(jnp.broadcast_to(x[None], (lax.axis_size(axis), *x.shape)), axis)


def local(positions, polarizability, seeds, dipoles, tile_mask):
    seeds = seeds.reshape(48, BEAD)
    pol = polarizability[None, :]
    own_v, own_mu = run_prep(seeds, dipoles.reshape(48, BEAD), positions, pol)
    w, xc, m = run_columns(broadcast_all(own_v, "row"), tile_mask)
    got_mu = broadcast_all(own_mu, "col")
    moments = run_moments(got_mu)
    t, f5, g7, xb, parts = run_build(got_mu, w, xc, m)
    own_next = run_first_own(exchange(parts, "col"), own_v)
    pieces = run_second(broadcast_all(own_next, "col"), t)
    field, own_adjoint = run_second_own(exchange(pieces, "row"), seeds, pol)
    out_r, out_c = run_gradient(broadcast_all(own_adjoint, "row"), moments, xb, f5, g7, xc)
    gradient = run_final(exchange(out_r, "col"), exchange(out_c, "row"))
    return (field.reshape(3, 16, BEAD), gradient)


def solution(mesh):
    in_specs = (
        P(None, ("row", "col")),
        P(("row", "col")),
        P(None, None, ("row", "col")),
        P(None, None, ("row", "col")),
        P("row", "col"),
    )
    out_specs = (P(None, None, ("row", "col")), P(None, ("row", "col")))
    return jax.shard_map(local, mesh=mesh, in_specs=in_specs, out_specs=out_specs, check_vma=False)
```

```python
import jax
import jax.numpy as jnp
from jax import lax
from jax.experimental import pallas as pl
from jax.experimental.pallas import tpu as pltpu
from jax.sharding import PartitionSpec as P

THOLE_DAMPING = 0.39
HIGHEST = lax.Precision.HIGHEST
F32 = jnp.float32
BF16 = jnp.bfloat16

BEAD = 56
NROW = 32
NCOL = 8
RB = NCOL * BEAD
CB = NROW * BEAD
LANE = 128
GEO = 48
PAIRS = ((0, 0), (1, 1), (2, 2), (0, 1), (0, 2), (1, 2))
VMEM_SPEC = pl.BlockSpec(memory_space=pltpu.VMEM)


def dot_f32(a, b, dims, precision=None):
    return lax.dot_general(a, b, (dims, ((), ())), precision=precision, preferred_element_type=F32)


def hi_lo(x):
    hi = x.astype(BF16).astype(F32)
    return hi, x - hi


def lane_ids(shape):
    return lax.broadcasted_iota(jnp.int32, shape, 1)


def vector_lanes(x):
    return jnp.where(lane_ids(x.shape) < GEO, x, 0.0)


def arranged(u, a, b):
    group = (lane_ids(u.shape) % 64) // 16
    if a == b:
        return jnp.where(group == a, u, 0.0)
    step = 16 * (b - a)
    down = pltpu.roll(u, LANE - step, 1)
    up = pltpu.roll(u, step, 1)
    return jnp.where(group == a, down, jnp.where(group == b, up, 0.0))


def unpack(got_ref, out_ref, blocks):
    for j in range(blocks):
        piece = got_ref[j]
        out_ref[j * BEAD : j * BEAD + 32, :] = piece
        out_ref[j * BEAD + 32 : (j + 1) * BEAD, :] = pltpu.roll(piece[0:24], 64, 1)


def prep_kernel(x_ref, own_ref, v_ref, mu_ref, mask_ref):
    pol = x_ref[99:100, :]
    row = lax.broadcasted_iota(jnp.int32, (16, BEAD), 0)
    geo = jnp.where(row == 3, lax.rsqrt(pol), jnp.where(row == 4, pol, 0.0))
    for i in range(3):
        geo = jnp.where(row == i, x_ref[96 + i : 97 + i, :], geo)
    both = jnp.concatenate([pol * x_ref[0:48, :], geo, x_ref[48:96, :], geo], axis=0)
    both = jnp.concatenate([both, jnp.zeros((LANE, LANE - BEAD), F32)], axis=1)
    turned = both.T
    swapped = pltpu.roll(turned, 64, 1)
    left = lane_ids((32, LANE)) < 64
    own = jnp.where(left, turned[0:32], swapped[32:64])
    own_ref[...] = own
    for k in range(NROW):
        v_ref[k] = own
    own = jnp.where(left, swapped[0:32], turned[32:64])
    for k in range(NCOL):
        mu_ref[k] = own
    mask_ref[...] = x_ref[104:112, 0:NROW]


def prepare_columns(got_ref, mask_ref, w_ref, xc_ref, m_ref, g_ref):
    unpack(got_ref, g_ref, NROW)
    for k in range(CB // 256):
        rows = pl.ds(k * 256, 256)
        g = g_ref[rows, :]
        xc_ref[:, rows] = g.T[GEO : GEO + 8]
        hi, lo = hi_lo(vector_lanes(g))
        u = hi + pltpu.roll(lo, 64, 1)
        for n, (a, b) in enumerate(PAIRS):
            w_ref[n, rows, :] = arranged(u, a, b).astype(BF16)
    block = lax.broadcasted_iota(jnp.int32, (NROW, CB), 1) // BEAD
    owner = lax.broadcasted_iota(jnp.int32, (NROW, CB), 0)
    chosen = (block == owner).astype(BF16)
    keep_all = dot_f32(mask_ref[...].astype(BF16), chosen, ((1,), (0,)))
    for k in range(NCOL):
        m_ref[k] = jnp.broadcast_to(keep_all[k : k + 1], (8, CB))


def prepare_moments(l_ref, g_ref):
    hi, lo = hi_lo(vector_lanes(g_ref[...]))
    hi = hi + pltpu.roll(hi, 64, 1)
    lo = lo + pltpu.roll(lo, 64, 1)
    for n, (p, q) in enumerate(PAIRS):
        scale = 2.0 if p == q else 1.0
        l_ref[n, :, 0:LANE] = (arranged(hi, p, q) * scale).astype(BF16)
        l_ref[n, :, LANE:] = (arranged(lo, p, q) * scale).astype(BF16)


def build_kernel(
    gotv_ref,
    gotm_ref,
    mask_ref,
    t_ref,
    f5_ref,
    g7_ref,
    xb_ref,
    xc_ref,
    l_ref,
    out_ref,
    gc_ref,
    g_ref,
    y_ref,
    w_ref,
    m_ref,
):
    prepare_columns(gotv_ref, mask_ref, w_ref, xc_ref, m_ref, gc_ref)
    unpack(gotm_ref, g_ref, NCOL)
    prepare_moments(l_ref, g_ref)
    for i in range(4):
        spread = jnp.broadcast_to(g_ref[:, GEO + i : GEO + i + 1], (RB, LANE))
        xb_ref[i] = spread * THOLE_DAMPING if i == 3 else spread

    def row_chunk(q, carry):
        r0 = pl.multiple_of(q * 16, 16)
        rows = pl.ds(r0, 16)
        xr, yr, zr, sr = (xb_ref[i, rows, :] for i in range(4))
        first = (2 * q) // 7
        second = (2 * q + 1) // 7
        for k in range(CB // LANE):
            cols = pl.ds(k * LANE, LANE)
            xc, yc, zc, sc = (jnp.broadcast_to(xc_ref[i : i + 1, cols], (16, LANE)) for i in range(4))
            keep = jnp.concatenate([m_ref[first, :, cols], m_ref[second, :, cols]], axis=0)
            dx, dy, dz = xr - xc, yr - yc, zr - zc
            r2 = dx * dx + dy * dy + dz * dz
            inv = lax.rsqrt(jnp.maximum(r2, 1e-12)) * keep
            v = (r2 * (r2 * inv)) * (sr * sc)
            e = jnp.exp(-v)
            ve = v * e
            one = 1.0 - e
            inv2 = inv * inv
            inv3 = inv2 * inv
            f3 = one * inv3
            inv5 = inv3 * inv2
            f5 = ((one - ve) * 3.0) * inv5
            g7 = inv2 * ((v * ve) * inv5 * 9.0 - 5.0 * f5)
            f5_ref[rows, cols] = f5
            g7_ref[rows, cols] = g7
            fx, fy, fz = f5 * dx, f5 * dy, f5 * dz
            parts = (fx * dx - f3, fy * dy - f3, fz * dz - f3, fx * dy, fx * dz, fy * dz)
            for n, t in enumerate(parts):
                hi = t.astype(BF16)
                t_ref[n, rows, cols] = hi
                t_ref[6 + n, rows, cols] = (t - hi.astype(F32)).astype(BF16)
        return carry

    lax.fori_loop(0, RB // 16, row_chunk, 0)
    total = dot_f32(t_ref[0], w_ref[0], ((1,), (0,)))
    for n in range(1, 12):
        total += dot_f32(t_ref[n], w_ref[n % 6], ((1,), (0,)))
    y_ref[...] = total + pltpu.roll(total, 64, 1)
    left = lane_ids((24, LANE)) < 64
    for k in range(NCOL):
        at = k * BEAD
        out_ref[k, 0:24, :] = jnp.where(left, y_ref[at : at + 24, :], y_ref[at + 32 : at + 56, :])
        out_ref[k, 24:32, :] = y_ref[at + 24 : at + 32, :]


def first_own_kernel(got_ref, v_ref, out_ref):
    y = got_ref[0]
    for k in range(1, NCOL):
        y = y + got_ref[k]
    v = v_ref[...]
    lanes = lane_ids((32, LANE))
    pol = jnp.where(
        lanes < 64,
        jnp.broadcast_to(v[:, GEO + 4 : GEO + 5], (32, LANE)),
        jnp.broadcast_to(v[:, 64 + GEO + 4 : 64 + GEO + 5], (32, LANE)),
    )
    own = jnp.where(lanes % 64 < GEO, v + pol * y, 0.0)
    for k in range(NCOL):
        out_ref[k] = own


def second_kernel(got_ref, t_ref, out_ref, g_ref, w_ref, y_ref):
    unpack(got_ref, g_ref, NCOL)
    hi, lo = hi_lo(vector_lanes(g_ref[...]))
    ut = (hi + pltpu.roll(lo, 64, 1)).T
    ut = jnp.concatenate([ut[0:48], ut[64:112]], axis=0)
    group = (lax.broadcasted_iota(jnp.int32, (96, RB), 0) % 48) // 16
    for n, (a, b) in enumerate(PAIRS):
        if a == b:
            w = jnp.where(group == a, ut, 0.0)
        else:
            step = 16 * (b - a)
            down = jnp.concatenate([ut[step:], ut[:step]], axis=0)
            up = jnp.concatenate([ut[96 - step :], ut[: 96 - step]], axis=0)
            w = jnp.where(group == a, down, jnp.where(group == b, up, 0.0))
        w_ref[n] = w.astype(BF16)
    for k in range(7):
        cols = pl.ds(k * 256, 256)
        total = jnp.zeros((96, 256), F32)
        for n in range(12):
            total += dot_f32(w_ref[n % 6], t_ref[n, :, cols], ((1,), (0,)))
        y_ref[:, cols] = total[0:48] + total[48:96]
    for j in range(NROW):
        out_ref[j, :, 0:BEAD] = y_ref[0:24, j * BEAD : (j + 1) * BEAD]
        out_ref[j, :, 64 : 64 + BEAD] = y_ref[24:48, j * BEAD : (j + 1) * BEAD]


def second_own_kernel(got_ref, seeds_ref, pol_ref, field_ref, next_ref):
    y = got_ref[0]
    for k in range(1, NROW):
        y = y + got_ref[k]
    y = jnp.concatenate([y, pltpu.roll(y, 64, 1)], axis=0)
    field = seeds_ref[...] + y[:, 0:BEAD]
    field_ref[...] = field
    vec = pol_ref[...] * field
    vec = jnp.concatenate([vec, jnp.zeros((48, LANE - BEAD), F32)], axis=1)
    turned = jnp.concatenate([vec, jnp.zeros((LANE - 48, LANE), F32)], axis=0).T
    left = lane_ids((32, LANE)) < 64
    own = jnp.where(left, turned[0:32], pltpu.roll(turned[32:64], 64, 1))
    for k in range(NROW):
        next_ref[k] = own


def gradient_kernel(
    got_ref, l_ref, xb_ref, f5_ref, g7_ref, xc_ref, or_ref, oc_ref, g_ref, m_ref, h_ref, racc_ref, cacc_ref
):
    unpack(got_ref, g_ref, NROW)
    for k in range(CB // 256):
        rows = pl.ds(k * 256, 256)
        hi, lo = hi_lo(vector_lanes(g_ref[rows, :]))
        u = (hi + pltpu.roll(lo, 64, 1)).astype(BF16)
        m_ref[rows, 0:LANE] = u
        m_ref[rows, LANE:] = u
    racc_ref[...] = jnp.zeros_like(racc_ref)

    def col_chunk(k, carry):
        c0 = pl.multiple_of(k * 256, 256)
        cols = pl.ds(c0, 256)
        for n in range(6):
            h_ref[n] = dot_f32(l_ref[n], m_ref[cols, :], ((1,), (1,)))
        xc, yc, zc = (jnp.broadcast_to(xc_ref[i : i + 1, cols], (8, 256)) for i in range(3))

        def rows_step(t, acc):
            r0 = pl.multiple_of(t * 8, 8)
            rows = pl.ds(r0, 8)
            xr, yr, zr = (jnp.concatenate([xb_ref[i, rows, :]] * 2, axis=1) for i in range(3))
            dx, dy, dz = xr - xc, yr - yc, zr - zc
            hxx, hyy, hzz, hxy, hxz, hyz = (h_ref[n, rows, :] for n in range(6))
            wx = hxx * dx + hxy * dy + hxz * dz
            wy = hxy * dx + hyy * dy + hyz * dz
            wz = hxz * dx + hyz * dy + hzz * dz
            f5 = f5_ref[rows, cols]
            e = g7_ref[rows, cols] * (wx * dx + wy * dy + wz * dz) + f5 * (hxx + hyy + hzz)
            f52 = f5 + f5
            out = []
            for i, (d, w) in enumerate(((dx, wx), (dy, wy), (dz, wz))):
                s = e * d + f52 * w
                racc_ref[i, rows, :] += s[:, 0:LANE] + s[:, LANE:]
                out.append(acc[i] + s)
            return tuple(out)

        zero = jnp.zeros((8, 256), F32)
        acc = lax.fori_loop(0, RB // 8, rows_step, (zero, zero, zero), unroll=4)
        for i in range(3):
            cacc_ref[i : i + 1, cols] = -0.5 * jnp.sum(acc[i], axis=0, keepdims=True)
        return carry

    lax.fori_loop(0, CB // 256, col_chunk, 0)
    ones = jnp.full((8, LANE), 0.5, F32)
    row = lax.broadcasted_iota(jnp.int32, (8, RB), 0)
    total = jnp.zeros((8, RB), F32)
    for i in range(3):
        part = dot_f32(ones, racc_ref[i], ((1,), (1,)), HIGHEST)
        total = jnp.where(row == i, part, total)
    for j in range(NCOL):
        or_ref[j, :, 0:BEAD] = total[:, j * BEAD : (j + 1) * BEAD]
    for j in range(NROW):
        oc_ref[j, :, 0:BEAD] = cacc_ref[:, j * BEAD : (j + 1) * BEAD]


def final_kernel(rgot_ref, cgot_ref, out_ref):
    total = rgot_ref[0]
    for k in range(1, NCOL):
        total = total + rgot_ref[k]
    for k in range(NROW):
        total = total + cgot_ref[k]
    out_ref[...] = total[0:3, 0:BEAD]


def call(kernel, outs, scratch, flops, limit_mib):
    return pl.pallas_call(
        kernel,
        out_shape=[jax.ShapeDtypeStruct(s, t) for s, t in outs],
        out_specs=[VMEM_SPEC] * len(outs),
        scratch_shapes=[pltpu.VMEM(s, t) for s, t in scratch],
        compiler_params=pltpu.CompilerParams(vmem_limit_bytes=limit_mib << 20),
        cost_estimate=pl.CostEstimate(flops=flops, bytes_accessed=1_000_000, transcendentals=0),
    )


def run_prep(x):
    outs = [((32, LANE), F32), ((NROW, 32, LANE), F32), ((NCOL, 32, LANE), F32), ((NCOL, NROW), F32)]
    return call(prep_kernel, outs, [], 100_000, 4)(x)


def run_build(gotv, gotm, mask):
    outs = [
        ((12, RB, CB), BF16),
        ((RB, CB), F32),
        ((RB, CB), F32),
        ((4, RB, LANE), F32),
        ((8, CB), F32),
        ((6, RB, 2 * LANE), BF16),
        ((NCOL, 32, LANE), F32),
    ]
    scratch = [
        ((CB, LANE), F32),
        ((RB, LANE), F32),
        ((RB, LANE), F32),
        ((6, CB, LANE), BF16),
        ((NCOL, 8, CB), F32),
    ]
    return call(build_kernel, outs, scratch, 400_000_000, 8)(gotv, gotm, mask)


def run_first_own(got, v):
    return call(first_own_kernel, [((NCOL, 32, LANE), F32)], [], 100_000, 4)(got, v)[0]


def run_second(got, t):
    scratch = [((RB, LANE), F32), ((6, 96, RB), BF16), ((48, CB), F32)]
    return call(second_kernel, [((NROW, 24, LANE), F32)], scratch, 200_000_000, 6)(got, t)[0]


def run_second_own(got, seeds, pol):
    outs = [((48, BEAD), F32), ((NROW, 32, LANE), F32)]
    return call(second_own_kernel, outs, [], 100_000, 4)(got, seeds, pol)


def run_gradient(got, l, xb, f5, g7, xc):
    outs = [((NCOL, 8, LANE), F32), ((NROW, 8, LANE), F32)]
    scratch = [
        ((CB, LANE), F32),
        ((CB, 2 * LANE), BF16),
        ((6, RB, 256), F32),
        ((3, RB, LANE), F32),
        ((8, CB), F32),
    ]
    return call(gradient_kernel, outs, scratch, 300_000_000, 12)(got, l, xb, f5, g7, xc)


def run_final(rgot, cgot):
    return call(final_kernel, [((3, BEAD), F32)], [], 100_000, 4)(rgot, cgot)[0]


def exchange(x, axis):
    return lax.all_to_all(x, axis, 0, 0, tiled=True)


def local(positions, polarizability, seeds, dipoles, tile_mask):
    seeds = seeds.reshape(48, BEAD)
    pol = polarizability[None, :]
    mask = jnp.pad(tile_mask.astype(F32), ((0, 0), (0, BEAD - NROW)))
    blank = jnp.zeros((4, BEAD), F32)
    own_v, all_v, all_mu, mask = run_prep(
        jnp.concatenate([seeds, dipoles.reshape(48, BEAD), positions, pol, blank, mask], axis=0)
    )
    got_v = exchange(all_v, "row")
    got_mu = exchange(all_mu, "col")
    t, f5, g7, xb, xc, moments, parts = run_build(got_v, got_mu, mask)
    own_next = run_first_own(exchange(parts, "col"), own_v)
    pieces = run_second(exchange(own_next, "col"), t)
    field, own_adjoint = run_second_own(exchange(pieces, "row"), seeds, pol)
    out_r, out_c = run_gradient(exchange(own_adjoint, "row"), moments, xb, f5, g7, xc)
    gradient = run_final(exchange(out_r, "col"), exchange(out_c, "row"))
    return (field.reshape(3, 16, BEAD), gradient)


def solution(mesh):
    in_specs = (
        P(None, ("row", "col")),
        P(("row", "col")),
        P(None, None, ("row", "col")),
        P(None, None, ("row", "col")),
        P("row", "col"),
    )
    out_specs = (P(None, None, ("row", "col")), P(None, ("row", "col")))
    return jax.shard_map(local, mesh=mesh, in_specs=in_specs, out_specs=out_specs, check_vma=False)
```

```python
import jax
import jax.numpy as jnp
from jax import lax
from jax.experimental import pallas as pl
from jax.experimental.pallas import tpu as pltpu
from jax.sharding import Mesh
from jax.sharding import PartitionSpec as P

THOLE_DAMPING = 0.39
HIGHEST = lax.Precision.HIGHEST
F32 = jnp.float32
BF16 = jnp.bfloat16

BEAD = 56
NROW = 32
NCOL = 8
RB = NCOL * BEAD
CB = NROW * BEAD
LANE = 128
GEO = 48
AXES = ("zl", "y", "x", "zh", "c")
SIZES = (2, 4, 4, 4, 2)
ROWS_OVER = ("zl", "zh")
COLS_OVER = ("c", "y", "x")
FREE = (53, 117)
PAIRS = ((0, 0), (1, 1), (2, 2), (0, 1), (0, 2), (1, 2))
VMEM_SPEC = pl.BlockSpec(memory_space=pltpu.VMEM)


def dot_f32(a, b, dims, precision=None):
    return lax.dot_general(a, b, (dims, ((), ())), precision=precision, preferred_element_type=F32)


def hi_lo(x):
    hi = x.astype(BF16).astype(F32)
    return hi, x - hi


def lane_ids(shape):
    return lax.broadcasted_iota(jnp.int32, shape, 1)


def vector_lanes(x):
    return jnp.where(lane_ids(x.shape) < GEO, x, 0.0)


def arranged(u, a, b):
    group = (lane_ids(u.shape) % 64) // 16
    if a == b:
        return jnp.where(group == a, u, 0.0)
    step = 16 * (b - a)
    down = pltpu.roll(u, LANE - step, 1)
    up = pltpu.roll(u, step, 1)
    return jnp.where(group == a, down, jnp.where(group == b, up, 0.0))


def unpack(got_ref, out_ref, blocks):
    for j in range(blocks):
        piece = got_ref[j]
        out_ref[j * BEAD : j * BEAD + 32, :] = piece
        out_ref[j * BEAD + 32 : (j + 1) * BEAD, :] = pltpu.roll(piece[0:24], 64, 1)


def place():
    return lax.axis_index("zh"), lax.axis_index("y") * 4 + lax.axis_index("x")


def free_slot(lane):
    left = (lane >= FREE[0]) & (lane < FREE[0] + 8)
    right = (lane >= FREE[1]) & (lane < FREE[1] + 8)
    return jnp.where(left, lane - FREE[0], jnp.where(right, lane - FREE[1] + 8, -1))


def unpack_dense(got_ref, out_ref, blocks):
    lanes = lane_ids((8, LANE))
    for j in range(blocks):
        piece = got_ref[j]
        at = j * BEAD
        out_ref[at : at + 24, :] = piece
        out_ref[at + 24 : at + 48, :] = pltpu.roll(piece, 64, 1)
        first, second, third = (
            pltpu.roll(piece[8 * i : 8 * i + 8], 80 + 16 * i, 1) for i in range(3)
        )
        last = jnp.where(lanes < 16, first, jnp.where(lanes < 32, second, third))
        out_ref[at + 48 : at + 56, :] = last


def prep_kernel(x_ref, own_ref, mu_ref):
    pol = x_ref[99:100, :]
    row = lax.broadcasted_iota(jnp.int32, (16, BEAD), 0)
    geo = jnp.where(row == 3, lax.rsqrt(pol), jnp.where(row == 4, pol, 0.0))
    for i in range(3):
        geo = jnp.where(row == i, x_ref[96 + i : 97 + i, :], geo)
    both = jnp.concatenate([pol * x_ref[0:48, :], geo, x_ref[48:96, :], geo], axis=0)
    both = jnp.concatenate([both, jnp.zeros((LANE, LANE - BEAD), F32)], axis=1)
    turned = both.T
    swapped = pltpu.roll(turned, 64, 1)
    left = lane_ids((32, LANE)) < 64
    own = jnp.where(left, turned[0:32], swapped[32:64])
    own_ref[...] = own
    own = jnp.where(left, swapped[0:32], turned[32:64])
    mask = x_ref[104:112, :].astype(BF16)
    column = lax.broadcasted_iota(jnp.int32, (BEAD, LANE), 0)
    slot = free_slot(lane_ids((BEAD, LANE)))
    for zl in range(2):
        chosen = ((slot >= 0) & (column == slot + 16 * zl)).astype(BF16)
        part = own[0:8] + dot_f32(mask, chosen, ((1,), (0,)))
        for zh in range(4):
            mu_ref[zl * 4 + zh, 0:8, :] = part
            mu_ref[zl * 4 + zh, 8:32, :] = own[8:32]


def relay_kernel(got_ref, own_ref, v_ref):
    zh = place()[0]
    slot = free_slot(lane_ids((8, LANE)))
    row = lax.broadcasted_iota(jnp.int32, (8, 8), 0)
    source = lax.broadcasted_iota(jnp.int32, (8, 8), 1)
    held = [jnp.where(slot >= 0, got_ref[zl * 4 + zh, 0:8, :], 0.0).astype(BF16) for zl in range(2)]
    own = own_ref[...]
    for core in range(2):
        part = own[0:8]
        for zl in range(2):
            chosen = ((row // 4 == zl) & (source == (row % 4) * 2 + core)).astype(BF16)
            part = part + dot_f32(chosen, held[zl], ((1,), (0,)))
        for yx in range(16):
            v_ref[core * 16 + yx, 0:8, :] = part
            v_ref[core * 16 + yx, 8:32, :] = own[8:32]


def prepare_columns(got_ref, w_ref, xc_ref, m_ref, g_ref):
    unpack(got_ref, g_ref, NROW)
    for k in range(CB // 256):
        rows = pl.ds(k * 256, 256)
        g = g_ref[rows, :]
        xc_ref[:, rows] = g.T[GEO : GEO + 8]
        hi, lo = hi_lo(vector_lanes(g))
        u = hi + pltpu.roll(lo, 64, 1)
        for n, (a, b) in enumerate(PAIRS):
            w_ref[n, rows, :] = arranged(u, a, b).astype(BF16)
    block = lax.broadcasted_iota(jnp.int32, (LANE, CB), 1) // BEAD
    slot = free_slot(lax.broadcasted_iota(jnp.int32, (LANE, CB), 0))
    here = place()[1]
    keep_all = jnp.zeros((NCOL, CB), F32)
    for core in range(2):
        held = got_ref[core * 16 + here, 0:8, :]
        held = jnp.where(free_slot(lane_ids((8, LANE))) >= 0, held, 0.0).astype(BF16)
        chosen = (block == core * 16 + slot).astype(BF16)
        keep_all = keep_all + dot_f32(held, chosen, ((1,), (0,)))
    for k in range(NCOL):
        m_ref[k] = jnp.broadcast_to(keep_all[k : k + 1], (8, CB))


def prepare_moments(l_ref, g_ref):
    hi, lo = hi_lo(vector_lanes(g_ref[...]))
    hi = hi + pltpu.roll(hi, 64, 1)
    lo = lo + pltpu.roll(lo, 64, 1)
    for n, (p, q) in enumerate(PAIRS):
        scale = 2.0 if p == q else 1.0
        l_ref[n, :, 0:LANE] = (arranged(hi, p, q) * scale).astype(BF16)
        l_ref[n, :, LANE:] = (arranged(lo, p, q) * scale).astype(BF16)


def build_kernel(
    gotv_ref,
    gotm_ref,
    t_ref,
    f5_ref,
    g7_ref,
    xb_ref,
    xc_ref,
    l_ref,
    out_ref,
    gc_ref,
    g_ref,
    y_ref,
    w_ref,
    m_ref,
):
    prepare_columns(gotv_ref, w_ref, xc_ref, m_ref, gc_ref)
    unpack(gotm_ref, g_ref, NCOL)
    prepare_moments(l_ref, g_ref)
    for i in range(4):
        spread = jnp.broadcast_to(g_ref[:, GEO + i : GEO + i + 1], (RB, LANE))
        xb_ref[i] = spread * THOLE_DAMPING if i == 3 else spread

    def row_chunk(q, carry):
        r0 = pl.multiple_of(q * 16, 16)
        rows = pl.ds(r0, 16)
        xr, yr, zr, sr = (xb_ref[i, rows, :] for i in range(4))
        first = (2 * q) // 7
        second = (2 * q + 1) // 7
        for k in range(CB // LANE):
            cols = pl.ds(k * LANE, LANE)
            xc, yc, zc, sc = (jnp.broadcast_to(xc_ref[i : i + 1, cols], (16, LANE)) for i in range(4))
            keep = jnp.concatenate([m_ref[first, :, cols], m_ref[second, :, cols]], axis=0)
            dx, dy, dz = xr - xc, yr - yc, zr - zc
            r2 = dx * dx + dy * dy + dz * dz
            inv = lax.rsqrt(jnp.maximum(r2, 1e-12)) * keep
            v = (r2 * (r2 * inv)) * (sr * sc)
            e = jnp.exp(-v)
            ve = v * e
            one = 1.0 - e
            inv2 = inv * inv
            inv3 = inv2 * inv
            f3 = one * inv3
            inv5 = inv3 * inv2
            f5 = ((one - ve) * 3.0) * inv5
            g7 = inv2 * ((v * ve) * inv5 * 9.0 - 5.0 * f5)
            f5_ref[rows, cols] = f5
            g7_ref[rows, cols] = g7
            fx, fy, fz = f5 * dx, f5 * dy, f5 * dz
            parts = (fx * dx - f3, fy * dy - f3, fz * dz - f3, fx * dy, fx * dz, fy * dz)
            for n, t in enumerate(parts):
                hi = t.astype(BF16)
                t_ref[n, rows, cols] = hi
                t_ref[6 + n, rows, cols] = (t - hi.astype(F32)).astype(BF16)
        return carry

    lax.fori_loop(0, RB // 16, row_chunk, 0)
    total = dot_f32(t_ref[0], w_ref[0], ((1,), (0,)))
    for n in range(1, 12):
        total += dot_f32(t_ref[n], w_ref[n % 6], ((1,), (0,)))
    y_ref[...] = total + pltpu.roll(total, 64, 1)
    left = lane_ids((24, LANE)) < 64
    for k in range(NCOL):
        at = k * BEAD
        out_ref[k, 0:24, :] = jnp.where(left, y_ref[at : at + 24, :], y_ref[at + 32 : at + 56, :])
        out_ref[k, 24:32, :] = y_ref[at + 24 : at + 32, :]


def first_own_kernel(got_ref, v_ref, out_ref):
    y = got_ref[0]
    for k in range(1, NCOL):
        y = y + got_ref[k]
    v = v_ref[...]
    lanes = lane_ids((32, LANE))
    pol = jnp.where(
        lanes < 64,
        jnp.broadcast_to(v[:, GEO + 4 : GEO + 5], (32, LANE)),
        jnp.broadcast_to(v[:, 64 + GEO + 4 : 64 + GEO + 5], (32, LANE)),
    )
    own = jnp.where(lanes % 64 < GEO, v + pol * y, 0.0)
    for k in range(NCOL):
        out_ref[k] = own


def second_kernel(got_ref, t_ref, out_ref, g_ref, w_ref, y_ref):
    unpack(got_ref, g_ref, NCOL)
    hi, lo = hi_lo(vector_lanes(g_ref[...]))
    ut = (hi + pltpu.roll(lo, 64, 1)).T
    ut = jnp.concatenate([ut[0:48], ut[64:112]], axis=0)
    group = (lax.broadcasted_iota(jnp.int32, (96, RB), 0) % 48) // 16
    for n, (a, b) in enumerate(PAIRS):
        if a == b:
            w = jnp.where(group == a, ut, 0.0)
        else:
            step = 16 * (b - a)
            down = jnp.concatenate([ut[step:], ut[:step]], axis=0)
            up = jnp.concatenate([ut[96 - step :], ut[: 96 - step]], axis=0)
            w = jnp.where(group == a, down, jnp.where(group == b, up, 0.0))
        w_ref[n] = w.astype(BF16)
    for k in range(7):
        cols = pl.ds(k * 256, 256)
        total = jnp.zeros((96, 256), F32)
        for n in range(12):
            total += dot_f32(w_ref[n % 6], t_ref[n, :, cols], ((1,), (0,)))
        y_ref[:, cols] = total[0:48] + total[48:96]
    for j in range(NROW):
        out_ref[j, :, 0:BEAD] = y_ref[0:24, j * BEAD : (j + 1) * BEAD]
        out_ref[j, :, 64 : 64 + BEAD] = y_ref[24:48, j * BEAD : (j + 1) * BEAD]


def second_own_kernel(got_ref, seeds_ref, pol_ref, field_ref, next_ref):
    y = got_ref[0]
    for k in range(1, NROW):
        y = y + got_ref[k]
    y = jnp.concatenate([y, pltpu.roll(y, 64, 1)], axis=0)
    field = seeds_ref[...] + y[:, 0:BEAD]
    field_ref[...] = field
    vec = pol_ref[...] * field
    vec = jnp.concatenate([vec, jnp.zeros((48, LANE - BEAD), F32)], axis=1)
    turned = jnp.concatenate([vec, jnp.zeros((LANE - 48, LANE), F32)], axis=0).T
    lanes = lane_ids((24, LANE))
    last = turned[48:56]
    last = jnp.concatenate([pltpu.roll(last, shift, 1) for shift in (48, 32, 16)], axis=0)
    own = jnp.where(lanes >= 64, pltpu.roll(turned[24:48], 64, 1), last)
    own = jnp.where(lanes < 48, turned[0:24], own)
    for k in range(NROW):
        next_ref[k] = own


def gradient_kernel(
    got_ref, l_ref, xb_ref, f5_ref, g7_ref, xc_ref, or_ref, oc_ref, g_ref, m_ref, h_ref, racc_ref, cacc_ref
):
    unpack_dense(got_ref, g_ref, NROW)
    for k in range(CB // 256):
        rows = pl.ds(k * 256, 256)
        hi, lo = hi_lo(vector_lanes(g_ref[rows, :]))
        u = (hi + pltpu.roll(lo, 64, 1)).astype(BF16)
        m_ref[rows, 0:LANE] = u
        m_ref[rows, LANE:] = u
    racc_ref[...] = jnp.zeros_like(racc_ref)

    def col_chunk(k, carry):
        c0 = pl.multiple_of(k * 256, 256)
        cols = pl.ds(c0, 256)
        for n in range(6):
            h_ref[n] = dot_f32(l_ref[n], m_ref[cols, :], ((1,), (1,)))
        xc, yc, zc = (jnp.broadcast_to(xc_ref[i : i + 1, cols], (8, 256)) for i in range(3))

        def rows_step(t, acc):
            r0 = pl.multiple_of(t * 8, 8)
            rows = pl.ds(r0, 8)
            xr, yr, zr = (jnp.concatenate([xb_ref[i, rows, :]] * 2, axis=1) for i in range(3))
            dx, dy, dz = xr - xc, yr - yc, zr - zc
            hxx, hyy, hzz, hxy, hxz, hyz = (h_ref[n, rows, :] for n in range(6))
            wx = hxx * dx + hxy * dy + hxz * dz
            wy = hxy * dx + hyy * dy + hyz * dz
            wz = hxz * dx + hyz * dy + hzz * dz
            f5 = f5_ref[rows, cols]
            e = g7_ref[rows, cols] * (wx * dx + wy * dy + wz * dz) + f5 * (hxx + hyy + hzz)
            f52 = f5 + f5
            out = []
            for i, (d, w) in enumerate(((dx, wx), (dy, wy), (dz, wz))):
                s = e * d + f52 * w
                racc_ref[i, rows, :] += s[:, 0:LANE] + s[:, LANE:]
                out.append(acc[i] + s)
            return tuple(out)

        zero = jnp.zeros((8, 256), F32)
        acc = lax.fori_loop(0, RB // 8, rows_step, (zero, zero, zero), unroll=4)
        for i in range(3):
            cacc_ref[i : i + 1, cols] = -0.5 * jnp.sum(acc[i], axis=0, keepdims=True)
        return carry

    lax.fori_loop(0, CB // 256, col_chunk, 0)
    ones = jnp.full((8, LANE), 0.5, F32)
    row = lax.broadcasted_iota(jnp.int32, (8, RB), 0)
    total = jnp.zeros((8, RB), F32)
    for i in range(3):
        part = dot_f32(ones, racc_ref[i], ((1,), (1,)), HIGHEST)
        total = jnp.where(row == i, part, total)
    for j in range(NCOL):
        or_ref[j, :, 0:BEAD] = total[:, j * BEAD : (j + 1) * BEAD]
    for j in range(NROW):
        oc_ref[j, :, 0:BEAD] = cacc_ref[:, j * BEAD : (j + 1) * BEAD]


def final_kernel(rgot_ref, cgot_ref, out_ref):
    total = rgot_ref[0]
    for k in range(1, NCOL):
        total = total + rgot_ref[k]
    for k in range(NROW):
        total = total + cgot_ref[k]
    out_ref[...] = total[0:3, 0:BEAD]


def call(kernel, outs, scratch, flops, limit_mib):
    return pl.pallas_call(
        kernel,
        out_shape=[jax.ShapeDtypeStruct(s, t) for s, t in outs],
        out_specs=[VMEM_SPEC] * len(outs),
        scratch_shapes=[pltpu.VMEM(s, t) for s, t in scratch],
        compiler_params=pltpu.CompilerParams(vmem_limit_bytes=limit_mib << 20),
        cost_estimate=pl.CostEstimate(flops=flops, bytes_accessed=1_000_000, transcendentals=0),
    )


def run_prep(x):
    return call(prep_kernel, [((32, LANE), F32), ((NCOL, 32, LANE), F32)], [], 100_000, 4)(x)


def run_relay(got, own):
    return call(relay_kernel, [((NROW, 32, LANE), F32)], [], 100_000, 4)(got, own)[0]


def run_build(gotv, gotm):
    outs = [
        ((12, RB, CB), BF16),
        ((RB, CB), F32),
        ((RB, CB), F32),
        ((4, RB, LANE), F32),
        ((8, CB), F32),
        ((6, RB, 2 * LANE), BF16),
        ((NCOL, 32, LANE), F32),
    ]
    scratch = [
        ((CB, LANE), F32),
        ((RB, LANE), F32),
        ((RB, LANE), F32),
        ((6, CB, LANE), BF16),
        ((NCOL, 8, CB), F32),
    ]
    return call(build_kernel, outs, scratch, 400_000_000, 8)(gotv, gotm)


def run_first_own(got, v):
    return call(first_own_kernel, [((NCOL, 32, LANE), F32)], [], 100_000, 4)(got, v)[0]


def run_second(got, t):
    scratch = [((RB, LANE), F32), ((6, 96, RB), BF16), ((48, CB), F32)]
    return call(second_kernel, [((NROW, 24, LANE), F32)], scratch, 200_000_000, 6)(got, t)[0]


def run_second_own(got, seeds, pol):
    outs = [((48, BEAD), F32), ((NROW, 24, LANE), F32)]
    return call(second_own_kernel, outs, [], 100_000, 4)(got, seeds, pol)


def run_gradient(got, l, xb, f5, g7, xc):
    outs = [((NCOL, 8, LANE), F32), ((NROW, 8, LANE), F32)]
    scratch = [
        ((CB, LANE), F32),
        ((CB, 2 * LANE), BF16),
        ((6, RB, 256), F32),
        ((3, RB, LANE), F32),
        ((8, CB), F32),
    ]
    return call(gradient_kernel, outs, scratch, 300_000_000, 12)(got, l, xb, f5, g7, xc)


def run_final(rgot, cgot):
    return call(final_kernel, [((3, BEAD), F32)], [], 100_000, 4)(rgot, cgot)[0]


def exchange(x, axis):
    return lax.all_to_all(x, axis, 0, 0, tiled=True)


def local(positions, polarizability, seeds, dipoles, tile_mask):
    seeds = seeds.reshape(48, BEAD)
    pol = polarizability[None, :]
    mask = jnp.pad(tile_mask.astype(F32), ((0, 0), (0, BEAD - NROW)))
    blank = jnp.zeros((4, BEAD), F32)
    own_v, all_mu = run_prep(
        jnp.concatenate([seeds, dipoles.reshape(48, BEAD), positions, pol, blank, mask], axis=0)
    )
    got_mu = exchange(all_mu, ROWS_OVER)
    got_v = exchange(run_relay(got_mu, own_v), COLS_OVER)
    t, f5, g7, xb, xc, moments, parts = run_build(got_v, got_mu)
    own_next = run_first_own(exchange(parts, ROWS_OVER), own_v)
    pieces = run_second(exchange(own_next, ROWS_OVER), t)
    field, own_adjoint = run_second_own(exchange(pieces, COLS_OVER), seeds, pol)
    out_r, out_c = run_gradient(exchange(own_adjoint, COLS_OVER), moments, xb, f5, g7, xc)
    gradient = run_final(exchange(out_r, ROWS_OVER), exchange(out_c, COLS_OVER))
    return (field.reshape(3, 16, BEAD), gradient)


def solution(mesh):
    named = Mesh(mesh.devices.reshape(SIZES), AXES)
    in_specs = (P(None, AXES), P(AXES), P(None, None, AXES), P(None, None, AXES), P(AXES[:3], AXES[3:]))
    out_specs = (P(None, None, AXES), P(None, AXES))
    return jax.shard_map(local, mesh=named, in_specs=in_specs, out_specs=out_specs, check_vma=False)
```

```python
import jax
import jax.numpy as jnp
from jax import lax
from jax.experimental import pallas as pl
from jax.experimental.pallas import tpu as pltpu
from jax.sharding import Mesh
from jax.sharding import PartitionSpec as P

THOLE_DAMPING = 0.39
HIGHEST = lax.Precision.HIGHEST
F32 = jnp.float32
BF16 = jnp.bfloat16

BEAD = 56
NROW = 32
NCOL = 8
RB = NCOL * BEAD
CB = NROW * BEAD
LANE = 128
GEO = 48
AXES = ("zl", "y", "x", "zh", "c")
SIZES = (2, 4, 4, 4, 2)
ROWS_OVER = ("zl", "zh")
COLS_OVER = ("c", "y", "x")
FREE = (53, 117)
PAIRS = ((0, 0), (1, 1), (2, 2), (0, 1), (0, 2), (1, 2))
VMEM_SPEC = pl.BlockSpec(memory_space=pltpu.VMEM)


def dot_f32(a, b, dims, precision=None):
    return lax.dot_general(a, b, (dims, ((), ())), precision=precision, preferred_element_type=F32)


def hi_lo(x):
    hi = x.astype(BF16).astype(F32)
    return hi, x - hi


def lane_ids(shape):
    return lax.broadcasted_iota(jnp.int32, shape, 1)


def vector_lanes(x):
    return jnp.where(lane_ids(x.shape) < GEO, x, 0.0)


def arranged(u, a, b):
    group = (lane_ids(u.shape) % 64) // 16
    if a == b:
        return jnp.where(group == a, u, 0.0)
    step = 16 * (b - a)
    down = pltpu.roll(u, LANE - step, 1)
    up = pltpu.roll(u, step, 1)
    return jnp.where(group == a, down, jnp.where(group == b, up, 0.0))


def arranged_rows(vec, w_ref, cols):
    hi, lo = hi_lo(vec)
    u = jnp.concatenate([hi, lo], axis=0)
    group = (lax.broadcasted_iota(jnp.int32, u.shape, 0) % 48) // 16
    for n, (a, b) in enumerate(PAIRS):
        if a == b:
            w = jnp.where(group == a, u, 0.0)
        else:
            step = 16 * (b - a)
            down = jnp.concatenate([u[step:], u[:step]], axis=0)
            up = jnp.concatenate([u[96 - step :], u[: 96 - step]], axis=0)
            w = jnp.where(group == a, down, jnp.where(group == b, up, 0.0))
        w_ref[n, :, cols] = w.astype(BF16)


def unpack(got_ref, out_ref, blocks):
    for j in range(blocks):
        piece = got_ref[j]
        out_ref[j * BEAD : j * BEAD + 32, :] = piece
        out_ref[j * BEAD + 32 : (j + 1) * BEAD, :] = pltpu.roll(piece[0:24], 64, 1)


def place():
    return lax.axis_index("zh"), lax.axis_index("y") * 4 + lax.axis_index("x")


def free_slot(lane):
    left = (lane >= FREE[0]) & (lane < FREE[0] + 8)
    right = (lane >= FREE[1]) & (lane < FREE[1] + 8)
    return jnp.where(left, lane - FREE[0], jnp.where(right, lane - FREE[1] + 8, -1))


def unpack_dense(got_ref, out_ref, blocks):
    lanes = lane_ids((8, LANE))
    for j in range(blocks):
        piece = got_ref[j]
        at = j * BEAD
        out_ref[at : at + 24, :] = piece
        out_ref[at + 24 : at + 48, :] = pltpu.roll(piece, 64, 1)
        first, second, third = (
            pltpu.roll(piece[8 * i : 8 * i + 8], 80 + 16 * i, 1) for i in range(3)
        )
        last = jnp.where(lanes < 16, first, jnp.where(lanes < 32, second, third))
        out_ref[at + 48 : at + 56, :] = last


def prep_kernel(x_ref, own_ref, mu_ref):
    pol = x_ref[99:100, :]
    row = lax.broadcasted_iota(jnp.int32, (16, BEAD), 0)
    geo = jnp.where(row == 3, lax.rsqrt(pol), jnp.where(row == 4, pol, 0.0))
    for i in range(3):
        geo = jnp.where(row == i, x_ref[96 + i : 97 + i, :], geo)
    both = jnp.concatenate([pol * x_ref[0:48, :], geo, x_ref[48:96, :], geo], axis=0)
    both = jnp.concatenate([both, jnp.zeros((LANE, LANE - BEAD), F32)], axis=1)
    turned = both.T
    swapped = pltpu.roll(turned, 64, 1)
    left = lane_ids((32, LANE)) < 64
    own = jnp.where(left, turned[0:32], swapped[32:64])
    own_ref[...] = own
    own = jnp.where(left, swapped[0:32], turned[32:64])
    mask = x_ref[104:112, :].astype(BF16)
    column = lax.broadcasted_iota(jnp.int32, (BEAD, LANE), 0)
    slot = free_slot(lane_ids((BEAD, LANE)))
    for zl in range(2):
        chosen = ((slot >= 0) & (column == slot + 16 * zl)).astype(BF16)
        part = own[0:8] + dot_f32(mask, chosen, ((1,), (0,)))
        for zh in range(4):
            mu_ref[zl * 4 + zh, 0:8, :] = part
            mu_ref[zl * 4 + zh, 8:32, :] = own[8:32]


def relay_kernel(got_ref, own_ref, v_ref):
    zh = place()[0]
    slot = free_slot(lane_ids((8, LANE)))
    row = lax.broadcasted_iota(jnp.int32, (8, 8), 0)
    source = lax.broadcasted_iota(jnp.int32, (8, 8), 1)
    held = [jnp.where(slot >= 0, got_ref[zl * 4 + zh, 0:8, :], 0.0).astype(BF16) for zl in range(2)]
    own = own_ref[...]
    for core in range(2):
        part = own[0:8]
        for zl in range(2):
            chosen = ((row // 4 == zl) & (source == (row % 4) * 2 + core)).astype(BF16)
            part = part + dot_f32(chosen, held[zl], ((1,), (0,)))
        for yx in range(16):
            v_ref[core * 16 + yx, 0:8, :] = part
            v_ref[core * 16 + yx, 8:32, :] = own[8:32]


def prepare_columns(got_ref, w_ref, xc_ref, m_ref, g_ref):
    unpack(got_ref, g_ref, NROW)
    for k in range(CB // 256):
        cols = pl.ds(k * 256, 256)
        turned = g_ref[cols, :].T
        xc_ref[:, cols] = turned[GEO : GEO + 8]
        arranged_rows(turned[0:48], w_ref, cols)
    block = lax.broadcasted_iota(jnp.int32, (LANE, CB), 1) // BEAD
    slot = free_slot(lax.broadcasted_iota(jnp.int32, (LANE, CB), 0))
    here = place()[1]
    keep_all = jnp.zeros((NCOL, CB), F32)
    for core in range(2):
        held = got_ref[core * 16 + here, 0:8, :]
        held = jnp.where(free_slot(lane_ids((8, LANE))) >= 0, held, 0.0).astype(BF16)
        chosen = (block == core * 16 + slot).astype(BF16)
        keep_all = keep_all + dot_f32(held, chosen, ((1,), (0,)))
    for k in range(NCOL):
        m_ref[k] = jnp.broadcast_to(keep_all[k : k + 1], (8, CB))


def prepare_moments(l_ref, g_ref):
    hi, lo = hi_lo(vector_lanes(g_ref[...]))
    hi = hi + pltpu.roll(hi, 64, 1)
    lo = lo + pltpu.roll(lo, 64, 1)
    for n, (p, q) in enumerate(PAIRS):
        scale = 2.0 if p == q else 1.0
        l_ref[n, :, 0:LANE] = (arranged(hi, p, q) * scale).astype(BF16)
        l_ref[n, :, LANE:] = (arranged(lo, p, q) * scale).astype(BF16)


def build_kernel(
    gotv_ref,
    gotm_ref,
    t_ref,
    f5_ref,
    g7_ref,
    xb_ref,
    xc_ref,
    l_ref,
    out_ref,
    gc_ref,
    g_ref,
    y_ref,
    w_ref,
    m_ref,
):
    prepare_columns(gotv_ref, w_ref, xc_ref, m_ref, gc_ref)
    unpack(gotm_ref, g_ref, NCOL)
    prepare_moments(l_ref, g_ref)
    for i in range(4):
        spread = jnp.broadcast_to(g_ref[:, GEO + i : GEO + i + 1], (RB, LANE))
        xb_ref[i] = spread * THOLE_DAMPING if i == 3 else spread

    def row_chunk(q, carry):
        r0 = pl.multiple_of(q * 16, 16)
        rows = pl.ds(r0, 16)
        xr, yr, zr, sr = (xb_ref[i, rows, :] for i in range(4))
        first = (2 * q) // 7
        second = (2 * q + 1) // 7
        for k in range(CB // LANE):
            cols = pl.ds(k * LANE, LANE)
            xc, yc, zc, sc = (jnp.broadcast_to(xc_ref[i : i + 1, cols], (16, LANE)) for i in range(4))
            keep = jnp.concatenate([m_ref[first, :, cols], m_ref[second, :, cols]], axis=0)
            dx, dy, dz = xr - xc, yr - yc, zr - zc
            r2 = dx * dx + dy * dy + dz * dz
            inv = lax.rsqrt(jnp.maximum(r2, 1e-12)) * keep
            v = (r2 * (r2 * inv)) * (sr * sc)
            e = jnp.exp(-v)
            ve = v * e
            one = 1.0 - e
            inv2 = inv * inv
            inv3 = inv2 * inv
            f3 = one * inv3
            inv5 = inv3 * inv2
            f5 = ((one - ve) * 3.0) * inv5
            g7 = inv2 * ((v * ve) * inv5 * 9.0 - 5.0 * f5)
            f5_ref[rows, cols] = f5
            g7_ref[rows, cols] = g7
            fx, fy, fz = f5 * dx, f5 * dy, f5 * dz
            parts = (fx * dx - f3, fy * dy - f3, fz * dz - f3, fx * dy, fx * dz, fy * dz)
            for n, t in enumerate(parts):
                hi = t.astype(BF16)
                t_ref[n, rows, cols] = hi
                t_ref[6 + n, rows, cols] = (t - hi.astype(F32)).astype(BF16)
        return carry

    lax.fori_loop(0, RB // 16, row_chunk, 0)
    total = dot_f32(w_ref[0], t_ref[0], ((1,), (1,)))
    for n in range(1, 12):
        total += dot_f32(w_ref[n % 6], t_ref[n], ((1,), (1,)))
    half = jnp.concatenate([total[0:48] + total[48:96], jnp.zeros((16, RB), F32)], axis=0)
    y_ref[...] = jnp.concatenate([half, half], axis=0).T
    left = lane_ids((24, LANE)) < 64
    for k in range(NCOL):
        at = k * BEAD
        out_ref[k, 0:24, :] = jnp.where(left, y_ref[at : at + 24, :], y_ref[at + 32 : at + 56, :])
        out_ref[k, 24:32, :] = y_ref[at + 24 : at + 32, :]


def first_own_kernel(got_ref, v_ref, out_ref):
    y = got_ref[0]
    for k in range(1, NCOL):
        y = y + got_ref[k]
    v = v_ref[...]
    lanes = lane_ids((32, LANE))
    pol = jnp.where(
        lanes < 64,
        jnp.broadcast_to(v[:, GEO + 4 : GEO + 5], (32, LANE)),
        jnp.broadcast_to(v[:, 64 + GEO + 4 : 64 + GEO + 5], (32, LANE)),
    )
    own = jnp.where(lanes % 64 < GEO, v + pol * y, 0.0)
    for k in range(NCOL):
        out_ref[k] = own


def second_kernel(got_ref, t_ref, out_ref, g_ref, w_ref, y_ref):
    unpack(got_ref, g_ref, NCOL)
    arranged_rows(g_ref[...].T[0:48], w_ref, slice(None))
    for k in range(7):
        cols = pl.ds(k * 256, 256)
        total = jnp.zeros((96, 256), F32)
        for n in range(12):
            total += dot_f32(w_ref[n % 6], t_ref[n, :, cols], ((1,), (0,)))
        y_ref[:, cols] = total[0:48] + total[48:96]
    for j in range(NROW):
        out_ref[j, :, 0:BEAD] = y_ref[0:24, j * BEAD : (j + 1) * BEAD]
        out_ref[j, :, 64 : 64 + BEAD] = y_ref[24:48, j * BEAD : (j + 1) * BEAD]


def second_own_kernel(got_ref, seeds_ref, pol_ref, field_ref, next_ref):
    y = got_ref[0]
    for k in range(1, NROW):
        y = y + got_ref[k]
    y = jnp.concatenate([y, pltpu.roll(y, 64, 1)], axis=0)
    field = seeds_ref[...] + y[:, 0:BEAD]
    field_ref[...] = field
    vec = pol_ref[...] * field
    vec = jnp.concatenate([vec, jnp.zeros((48, LANE - BEAD), F32)], axis=1)
    turned = jnp.concatenate([vec, jnp.zeros((LANE - 48, LANE), F32)], axis=0).T
    lanes = lane_ids((24, LANE))
    last = turned[48:56]
    last = jnp.concatenate([pltpu.roll(last, shift, 1) for shift in (48, 32, 16)], axis=0)
    own = jnp.where(lanes >= 64, pltpu.roll(turned[24:48], 64, 1), last)
    own = jnp.where(lanes < 48, turned[0:24], own)
    for k in range(NROW):
        next_ref[k] = own


def gradient_kernel(
    got_ref, l_ref, xb_ref, f5_ref, g7_ref, xc_ref, or_ref, oc_ref, g_ref, m_ref, h_ref, racc_ref, cacc_ref
):
    unpack_dense(got_ref, g_ref, NROW)
    for k in range(CB // 256):
        rows = pl.ds(k * 256, 256)
        hi, lo = hi_lo(vector_lanes(g_ref[rows, :]))
        u = (hi + pltpu.roll(lo, 64, 1)).astype(BF16)
        m_ref[rows, 0:LANE] = u
        m_ref[rows, LANE:] = u
    racc_ref[...] = jnp.zeros_like(racc_ref)

    def col_chunk(k, carry):
        c0 = pl.multiple_of(k * 256, 256)
        cols = pl.ds(c0, 256)
        for n in range(6):
            h_ref[n] = dot_f32(l_ref[n], m_ref[cols, :], ((1,), (1,)))
        xc, yc, zc = (jnp.broadcast_to(xc_ref[i : i + 1, cols], (8, 256)) for i in range(3))

        def rows_step(t, acc):
            r0 = pl.multiple_of(t * 8, 8)
            rows = pl.ds(r0, 8)
            xr, yr, zr = (jnp.concatenate([xb_ref[i, rows, :]] * 2, axis=1) for i in range(3))
            dx, dy, dz = xr - xc, yr - yc, zr - zc
            hxx, hyy, hzz, hxy, hxz, hyz = (h_ref[n, rows, :] for n in range(6))
            wx = hxx * dx + hxy * dy + hxz * dz
            wy = hxy * dx + hyy * dy + hyz * dz
            wz = hxz * dx + hyz * dy + hzz * dz
            f5 = f5_ref[rows, cols]
            e = g7_ref[rows, cols] * (wx * dx + wy * dy + wz * dz) + f5 * (hxx + hyy + hzz)
            f52 = f5 + f5
            out = []
            for i, (d, w) in enumerate(((dx, wx), (dy, wy), (dz, wz))):
                s = e * d + f52 * w
                racc_ref[i, rows, :] += s[:, 0:LANE] + s[:, LANE:]
                out.append(acc[i] + s)
            return tuple(out)

        zero = jnp.zeros((8, 256), F32)
        acc = lax.fori_loop(0, RB // 8, rows_step, (zero, zero, zero), unroll=4)
        for i in range(3):
            cacc_ref[i : i + 1, cols] = -0.5 * jnp.sum(acc[i], axis=0, keepdims=True)
        return carry

    lax.fori_loop(0, CB // 256, col_chunk, 0)
    ones = jnp.full((8, LANE), 0.5, F32)
    row = lax.broadcasted_iota(jnp.int32, (8, RB), 0)
    total = jnp.zeros((8, RB), F32)
    for i in range(3):
        part = dot_f32(ones, racc_ref[i], ((1,), (1,)), HIGHEST)
        total = jnp.where(row == i, part, total)
    for j in range(NCOL):
        or_ref[j, :, 0:BEAD] = total[:, j * BEAD : (j + 1) * BEAD]
    for j in range(NROW):
        oc_ref[j, :, 0:BEAD] = cacc_ref[:, j * BEAD : (j + 1) * BEAD]


def final_kernel(rgot_ref, cgot_ref, out_ref):
    total = rgot_ref[0]
    for k in range(1, NCOL):
        total = total + rgot_ref[k]
    for k in range(NROW):
        total = total + cgot_ref[k]
    out_ref[...] = total[0:3, 0:BEAD]


def call(kernel, outs, scratch, flops, limit_mib):
    return pl.pallas_call(
        kernel,
        out_shape=[jax.ShapeDtypeStruct(s, t) for s, t in outs],
        out_specs=[VMEM_SPEC] * len(outs),
        scratch_shapes=[pltpu.VMEM(s, t) for s, t in scratch],
        compiler_params=pltpu.CompilerParams(vmem_limit_bytes=limit_mib << 20),
        cost_estimate=pl.CostEstimate(flops=flops, bytes_accessed=1_000_000, transcendentals=0),
    )


def run_prep(x):
    return call(prep_kernel, [((32, LANE), F32), ((NCOL, 32, LANE), F32)], [], 100_000, 4)(x)


def run_relay(got, own):
    return call(relay_kernel, [((NROW, 32, LANE), F32)], [], 100_000, 4)(got, own)[0]


def run_build(gotv, gotm):
    outs = [
        ((12, RB, CB), BF16),
        ((RB, CB), F32),
        ((RB, CB), F32),
        ((4, RB, LANE), F32),
        ((8, CB), F32),
        ((6, RB, 2 * LANE), BF16),
        ((NCOL, 32, LANE), F32),
    ]
    scratch = [
        ((CB, LANE), F32),
        ((RB, LANE), F32),
        ((RB, LANE), F32),
        ((6, 96, CB), BF16),
        ((NCOL, 8, CB), F32),
    ]
    return call(build_kernel, outs, scratch, 400_000_000, 8)(gotv, gotm)


def run_first_own(got, v):
    return call(first_own_kernel, [((NCOL, 32, LANE), F32)], [], 100_000, 4)(got, v)[0]


def run_second(got, t):
    scratch = [((RB, LANE), F32), ((6, 96, RB), BF16), ((48, CB), F32)]
    return call(second_kernel, [((NROW, 24, LANE), F32)], scratch, 200_000_000, 6)(got, t)[0]


def run_second_own(got, seeds, pol):
    outs = [((48, BEAD), F32), ((NROW, 24, LANE), F32)]
    return call(second_own_kernel, outs, [], 100_000, 4)(got, seeds, pol)


def run_gradient(got, l, xb, f5, g7, xc):
    outs = [((NCOL, 8, LANE), F32), ((NROW, 8, LANE), F32)]
    scratch = [
        ((CB, LANE), F32),
        ((CB, 2 * LANE), BF16),
        ((6, RB, 256), F32),
        ((3, RB, LANE), F32),
        ((8, CB), F32),
    ]
    return call(gradient_kernel, outs, scratch, 300_000_000, 12)(got, l, xb, f5, g7, xc)


def run_final(rgot, cgot):
    return call(final_kernel, [((3, BEAD), F32)], [], 100_000, 4)(rgot, cgot)[0]


def exchange(x, axis):
    return lax.all_to_all(x, axis, 0, 0, tiled=True)


def local(positions, polarizability, seeds, dipoles, tile_mask):
    seeds = seeds.reshape(48, BEAD)
    pol = polarizability[None, :]
    mask = jnp.pad(tile_mask.astype(F32), ((0, 0), (0, BEAD - NROW)))
    blank = jnp.zeros((4, BEAD), F32)
    own_v, all_mu = run_prep(
        jnp.concatenate([seeds, dipoles.reshape(48, BEAD), positions, pol, blank, mask], axis=0)
    )
    got_mu = exchange(all_mu, ROWS_OVER)
    got_v = exchange(run_relay(got_mu, own_v), COLS_OVER)
    t, f5, g7, xb, xc, moments, parts = run_build(got_v, got_mu)
    own_next = run_first_own(exchange(parts, ROWS_OVER), own_v)
    pieces = run_second(exchange(own_next, ROWS_OVER), t)
    field, own_adjoint = run_second_own(exchange(pieces, COLS_OVER), seeds, pol)
    out_r, out_c = run_gradient(exchange(own_adjoint, COLS_OVER), moments, xb, f5, g7, xc)
    gradient = run_final(exchange(out_r, ROWS_OVER), exchange(out_c, COLS_OVER))
    return (field.reshape(3, 16, BEAD), gradient)


def solution(mesh):
    named = Mesh(mesh.devices.reshape(SIZES), AXES)
    in_specs = (P(None, AXES), P(AXES), P(None, None, AXES), P(None, None, AXES), P(AXES[:3], AXES[3:]))
    out_specs = (P(None, None, AXES), P(None, AXES))
    return jax.shard_map(local, mesh=named, in_specs=in_specs, out_specs=out_specs, check_vma=False)
```

```python
import jax
import jax.numpy as jnp
from jax import lax
from jax.experimental import pallas as pl
from jax.experimental.pallas import tpu as pltpu
from jax.sharding import Mesh
from jax.sharding import PartitionSpec as P

THOLE_DAMPING = 0.39
HIGHEST = lax.Precision.HIGHEST
F32 = jnp.float32
BF16 = jnp.bfloat16

BEAD = 56
NROW = 32
NCOL = 8
RB = NCOL * BEAD
CB = NROW * BEAD
LANE = 128
GEO = 48
AXES = ("zl", "y", "x", "zh", "c")
SIZES = (2, 4, 4, 4, 2)
ROWS_OVER = ("zl", "zh")
COLS_OVER = ("c", "y", "x")
FREE = (53, 117)
PAIRS = ((0, 0), (1, 1), (2, 2), (0, 1), (0, 2), (1, 2))
VMEM_SPEC = pl.BlockSpec(memory_space=pltpu.VMEM)


def dot_f32(a, b, dims, precision=None):
    return lax.dot_general(a, b, (dims, ((), ())), precision=precision, preferred_element_type=F32)


def hi_lo(x):
    hi = x.astype(BF16).astype(F32)
    return hi, x - hi


def lane_ids(shape):
    return lax.broadcasted_iota(jnp.int32, shape, 1)


def vector_lanes(x):
    return jnp.where(lane_ids(x.shape) < GEO, x, 0.0)


def arranged(u, a, b):
    group = (lane_ids(u.shape) % 64) // 16
    if a == b:
        return jnp.where(group == a, u, 0.0)
    step = 16 * (b - a)
    down = pltpu.roll(u, LANE - step, 1)
    up = pltpu.roll(u, step, 1)
    return jnp.where(group == a, down, jnp.where(group == b, up, 0.0))


def arranged_rows(vec, w_ref, cols):
    hi, lo = hi_lo(vec)
    u = jnp.concatenate([hi, lo], axis=0)
    group = (lax.broadcasted_iota(jnp.int32, u.shape, 0) % 48) // 16
    for n, (a, b) in enumerate(PAIRS):
        if a == b:
            w = jnp.where(group == a, u, 0.0)
        else:
            step = 16 * (b - a)
            down = jnp.concatenate([u[step:], u[:step]], axis=0)
            up = jnp.concatenate([u[96 - step :], u[: 96 - step]], axis=0)
            w = jnp.where(group == a, down, jnp.where(group == b, up, 0.0))
        w_ref[n, :, cols] = w.astype(BF16)


def unpack(got_ref, out_ref, blocks):
    for j in range(blocks):
        piece = got_ref[j]
        out_ref[j * BEAD : j * BEAD + 32, :] = piece
        out_ref[j * BEAD + 32 : (j + 1) * BEAD, :] = pltpu.roll(piece[0:24], 64, 1)


def place():
    return lax.axis_index("zh"), lax.axis_index("y") * 4 + lax.axis_index("x")


def free_slot(lane):
    left = (lane >= FREE[0]) & (lane < FREE[0] + 8)
    right = (lane >= FREE[1]) & (lane < FREE[1] + 8)
    return jnp.where(left, lane - FREE[0], jnp.where(right, lane - FREE[1] + 8, -1))


def unpack_dense(got_ref, out_ref, blocks):
    lanes = lane_ids((8, LANE))
    for j in range(blocks):
        piece = got_ref[j]
        at = j * BEAD
        out_ref[at : at + 24, :] = piece
        out_ref[at + 24 : at + 48, :] = pltpu.roll(piece, 64, 1)
        first, second, third = (
            pltpu.roll(piece[8 * i : 8 * i + 8], 80 + 16 * i, 1) for i in range(3)
        )
        last = jnp.where(lanes < 16, first, jnp.where(lanes < 32, second, third))
        out_ref[at + 48 : at + 56, :] = last


def prep_kernel(x_ref, own_ref, mu_ref):
    pol = x_ref[99:100, :]
    row = lax.broadcasted_iota(jnp.int32, (16, BEAD), 0)
    geo = jnp.where(row == 3, lax.rsqrt(pol), jnp.where(row == 4, pol, 0.0))
    for i in range(3):
        geo = jnp.where(row == i, x_ref[96 + i : 97 + i, :], geo)
    both = jnp.concatenate([pol * x_ref[0:48, :], geo, x_ref[48:96, :], geo], axis=0)
    both = jnp.concatenate([both, jnp.zeros((LANE, LANE - BEAD), F32)], axis=1)
    turned = both.T
    swapped = pltpu.roll(turned, 64, 1)
    left = lane_ids((32, LANE)) < 64
    own = jnp.where(left, turned[0:32], swapped[32:64])
    own_ref[...] = own
    own = jnp.where(left, swapped[0:32], turned[32:64])
    mask = x_ref[104:112, :].astype(BF16)
    column = lax.broadcasted_iota(jnp.int32, (BEAD, LANE), 0)
    slot = free_slot(lane_ids((BEAD, LANE)))
    for zl in range(2):
        chosen = ((slot >= 0) & (column == slot + 16 * zl)).astype(BF16)
        part = own[0:8] + dot_f32(mask, chosen, ((1,), (0,)))
        for zh in range(4):
            mu_ref[zl * 4 + zh, 0:8, :] = part
            mu_ref[zl * 4 + zh, 8:32, :] = own[8:32]


def relay_kernel(got_ref, own_ref, v_ref):
    zh = place()[0]
    slot = free_slot(lane_ids((8, LANE)))
    row = lax.broadcasted_iota(jnp.int32, (8, 8), 0)
    source = lax.broadcasted_iota(jnp.int32, (8, 8), 1)
    held = [jnp.where(slot >= 0, got_ref[zl * 4 + zh, 0:8, :], 0.0).astype(BF16) for zl in range(2)]
    own = own_ref[...]
    for core in range(2):
        part = own[0:8]
        for zl in range(2):
            chosen = ((row // 4 == zl) & (source == (row % 4) * 2 + core)).astype(BF16)
            part = part + dot_f32(chosen, held[zl], ((1,), (0,)))
        for yx in range(16):
            v_ref[core * 16 + yx, 0:8, :] = part
            v_ref[core * 16 + yx, 8:32, :] = own[8:32]


def prepare_columns(got_ref, w_ref, xc_ref, m_ref, g_ref):
    unpack(got_ref, g_ref, NROW)
    for k in range(CB // 256):
        cols = pl.ds(k * 256, 256)
        turned = g_ref[cols, :].T
        xc_ref[:, cols] = turned[GEO : GEO + 8]
        arranged_rows(turned[0:48], w_ref, cols)
    block = lax.broadcasted_iota(jnp.int32, (LANE, CB), 1) // BEAD
    slot = free_slot(lax.broadcasted_iota(jnp.int32, (LANE, CB), 0))
    here = place()[1]
    keep_all = jnp.zeros((NCOL, CB), F32)
    for core in range(2):
        held = got_ref[core * 16 + here, 0:8, :]
        held = jnp.where(free_slot(lane_ids((8, LANE))) >= 0, held, 0.0).astype(BF16)
        chosen = (block == core * 16 + slot).astype(BF16)
        keep_all = keep_all + dot_f32(held, chosen, ((1,), (0,)))
    for k in range(NCOL):
        m_ref[k] = jnp.broadcast_to(keep_all[k : k + 1], (8, CB))


def prepare_moments(l_ref, g_ref):
    hi, lo = hi_lo(vector_lanes(g_ref[...]))
    hi = hi + pltpu.roll(hi, 64, 1)
    lo = lo + pltpu.roll(lo, 64, 1)
    for n, (p, q) in enumerate(PAIRS):
        scale = 2.0 if p == q else 1.0
        l_ref[n, :, 0:LANE] = (arranged(hi, p, q) * scale).astype(BF16)
        l_ref[n, :, LANE:] = (arranged(lo, p, q) * scale).astype(BF16)


def build_kernel(
    gotv_ref,
    gotm_ref,
    t_ref,
    f5_ref,
    g7_ref,
    xb_ref,
    xc_ref,
    l_ref,
    out_ref,
    gc_ref,
    g_ref,
    y_ref,
    w_ref,
    m_ref,
):
    prepare_columns(gotv_ref, w_ref, xc_ref, m_ref, gc_ref)
    unpack(gotm_ref, g_ref, NCOL)
    prepare_moments(l_ref, g_ref)
    for i in range(4):
        spread = jnp.broadcast_to(g_ref[:, GEO + i : GEO + i + 1], (RB, LANE))
        xb_ref[i] = spread * THOLE_DAMPING if i == 3 else spread

    def row_chunk(q, carry):
        r0 = pl.multiple_of(q * 16, 16)
        rows = pl.ds(r0, 16)
        xr, yr, zr, sr = (xb_ref[i, rows, :] for i in range(4))
        first = (2 * q) // 7
        second = (2 * q + 1) // 7
        for k in range(CB // LANE):
            cols = pl.ds(k * LANE, LANE)
            xc, yc, zc, sc = (jnp.broadcast_to(xc_ref[i : i + 1, cols], (16, LANE)) for i in range(4))
            keep = jnp.concatenate([m_ref[first, :, cols], m_ref[second, :, cols]], axis=0)
            dx, dy, dz = xr - xc, yr - yc, zr - zc
            r2 = dx * dx + dy * dy + dz * dz
            inv = lax.rsqrt(jnp.maximum(r2, 1e-12)) * keep
            v = (r2 * (r2 * inv)) * (sr * sc)
            e = jnp.exp(-v)
            ve = v * e
            one = 1.0 - e
            inv2 = inv * inv
            inv3 = inv2 * inv
            f3 = one * inv3
            inv5 = inv3 * inv2
            f5 = ((one - ve) * 3.0) * inv5
            g7 = inv2 * ((v * ve) * inv5 * 9.0 - 5.0 * f5)
            f5_ref[rows, cols] = f5
            g7_ref[rows, cols] = g7
            fx, fy, fz = f5 * dx, f5 * dy, f5 * dz
            parts = (fx * dx - f3, fy * dy - f3, fz * dz - f3, fx * dy, fx * dz, fy * dz)
            for n, t in enumerate(parts):
                hi = t.astype(BF16)
                t_ref[n, rows, cols] = hi
                t_ref[6 + n, rows, cols] = (t - hi.astype(F32)).astype(BF16)
        return carry

    lax.fori_loop(0, RB // 16, row_chunk, 0)
    total = dot_f32(w_ref[0], t_ref[0], ((1,), (1,)))
    for n in range(1, 12):
        total += dot_f32(w_ref[n % 6], t_ref[n], ((1,), (1,)))
    half = jnp.concatenate([total[0:48] + total[48:96], jnp.zeros((16, RB), F32)], axis=0)
    y_ref[...] = jnp.concatenate([half, half], axis=0).T
    left = lane_ids((24, LANE)) < 64
    for k in range(NCOL):
        at = k * BEAD
        out_ref[k, 0:24, :] = jnp.where(left, y_ref[at : at + 24, :], y_ref[at + 32 : at + 56, :])
        out_ref[k, 24:32, :] = y_ref[at + 24 : at + 32, :]


def first_own_kernel(got_ref, v_ref, out_ref):
    y = got_ref[0]
    for k in range(1, NCOL):
        y = y + got_ref[k]
    v = v_ref[...]
    lanes = lane_ids((32, LANE))
    pol = jnp.where(
        lanes < 64,
        jnp.broadcast_to(v[:, GEO + 4 : GEO + 5], (32, LANE)),
        jnp.broadcast_to(v[:, 64 + GEO + 4 : 64 + GEO + 5], (32, LANE)),
    )
    own = jnp.where(lanes % 64 < GEO, v + pol * y, 0.0)
    for k in range(NCOL):
        out_ref[k] = own


def second_kernel(got_ref, t_ref, out_ref, g_ref, w_ref, y_ref):
    unpack(got_ref, g_ref, NCOL)
    arranged_rows(g_ref[...].T[0:48], w_ref, slice(None))
    for k in range(7):
        cols = pl.ds(k * 256, 256)
        total = jnp.zeros((96, 256), F32)
        for n in range(12):
            total += dot_f32(w_ref[n % 6], t_ref[n, :, cols], ((1,), (0,)))
        y_ref[:, cols] = total[0:48] + total[48:96]
    for j in range(NROW):
        out_ref[j, :, 0:BEAD] = y_ref[0:24, j * BEAD : (j + 1) * BEAD]
        out_ref[j, :, 64 : 64 + BEAD] = y_ref[24:48, j * BEAD : (j + 1) * BEAD]


def second_own_kernel(got_ref, seeds_ref, pol_ref, field_ref, next_ref):
    y = got_ref[0]
    for k in range(1, NROW):
        y = y + got_ref[k]
    y = jnp.concatenate([y, pltpu.roll(y, 64, 1)], axis=0)
    field = seeds_ref[...] + y[:, 0:BEAD]
    field_ref[...] = field
    vec = pol_ref[...] * field
    vec = jnp.concatenate([vec, jnp.zeros((48, LANE - BEAD), F32)], axis=1)
    turned = jnp.concatenate([vec, jnp.zeros((LANE - 48, LANE), F32)], axis=0).T
    lanes = lane_ids((24, LANE))
    last = turned[48:56]
    last = jnp.concatenate([pltpu.roll(last, shift, 1) for shift in (48, 32, 16)], axis=0)
    own = jnp.where(lanes >= 64, pltpu.roll(turned[24:48], 64, 1), last)
    own = jnp.where(lanes < 48, turned[0:24], own)
    for k in range(NROW):
        next_ref[k] = own


def gradient_kernel(
    got_ref, l_ref, xb_ref, f5_ref, g7_ref, xc_ref, or_ref, oc_ref, g_ref, m_ref, h_ref, racc_ref, cacc_ref
):
    unpack_dense(got_ref, g_ref, NROW)
    for k in range(CB // 256):
        rows = pl.ds(k * 256, 256)
        hi, lo = hi_lo(vector_lanes(g_ref[rows, :]))
        u = (hi + pltpu.roll(lo, 64, 1)).astype(BF16)
        m_ref[rows, 0:LANE] = u
        m_ref[rows, LANE:] = u
    racc_ref[...] = jnp.zeros_like(racc_ref)

    def col_chunk(k, carry):
        c0 = pl.multiple_of(k * 256, 256)
        cols = pl.ds(c0, 256)
        for n in range(6):
            h_ref[n] = dot_f32(l_ref[n], m_ref[cols, :], ((1,), (1,)))
        xc, yc, zc = (jnp.broadcast_to(xc_ref[i : i + 1, cols], (8, 256)) for i in range(3))

        def rows_step(t, acc):
            r0 = pl.multiple_of(t * 8, 8)
            rows = pl.ds(r0, 8)
            xr, yr, zr = (jnp.concatenate([xb_ref[i, rows, :]] * 2, axis=1) for i in range(3))
            dx, dy, dz = xr - xc, yr - yc, zr - zc
            hxx, hyy, hzz, hxy, hxz, hyz = (h_ref[n, rows, :] for n in range(6))
            wx = hxx * dx + hxy * dy + hxz * dz
            wy = hxy * dx + hyy * dy + hyz * dz
            wz = hxz * dx + hyz * dy + hzz * dz
            f5 = f5_ref[rows, cols]
            e = g7_ref[rows, cols] * (wx * dx + wy * dy + wz * dz) + f5 * (hxx + hyy + hzz)
            f52 = f5 + f5
            out = []
            for i, (d, w) in enumerate(((dx, wx), (dy, wy), (dz, wz))):
                s = e * d + f52 * w
                racc_ref[i, rows, :] += s[:, 0:LANE] + s[:, LANE:]
                out.append(acc[i] + s)
            return tuple(out)

        zero = jnp.zeros((8, 256), F32)
        acc = lax.fori_loop(0, RB // 8, rows_step, (zero, zero, zero), unroll=4)
        for i in range(3):
            cacc_ref[i : i + 1, cols] = -0.5 * jnp.sum(acc[i], axis=0, keepdims=True)
        return carry

    lax.fori_loop(0, CB // 256, col_chunk, 0)
    ones = jnp.full((8, LANE), 0.5, F32)
    row = lax.broadcasted_iota(jnp.int32, (8, RB), 0)
    total = jnp.zeros((8, RB), F32)
    for i in range(3):
        part = dot_f32(ones, racc_ref[i], ((1,), (1,)), HIGHEST)
        total = jnp.where(row == i, part, total)
    for j in range(NCOL):
        or_ref[j, :, 0:BEAD] = total[:, j * BEAD : (j + 1) * BEAD]
    for j in range(NROW):
        oc_ref[j, :, 0:BEAD] = cacc_ref[:, j * BEAD : (j + 1) * BEAD]


def final_kernel(rgot_ref, cgot_ref, out_ref):
    total = rgot_ref[0]
    for k in range(1, NCOL):
        total = total + rgot_ref[k]
    for k in range(NROW):
        total = total + cgot_ref[k]
    out_ref[...] = total[0:3, 0:BEAD]


def call(kernel, outs, scratch, flops, limit_mib):
    return pl.pallas_call(
        kernel,
        out_shape=[jax.ShapeDtypeStruct(s, t) for s, t in outs],
        out_specs=[VMEM_SPEC] * len(outs),
        scratch_shapes=[pltpu.VMEM(s, t) for s, t in scratch],
        compiler_params=pltpu.CompilerParams(vmem_limit_bytes=limit_mib << 20),
        cost_estimate=pl.CostEstimate(flops=flops, bytes_accessed=1_000_000, transcendentals=0),
    )


def run_prep(x):
    return call(prep_kernel, [((32, LANE), F32), ((NCOL, 32, LANE), F32)], [], 100_000, 4)(x)


def run_relay(got, own):
    return call(relay_kernel, [((NROW, 32, LANE), F32)], [], 100_000, 4)(got, own)[0]


def run_build(gotv, gotm):
    outs = [
        ((12, RB, CB), BF16),
        ((RB, CB), F32),
        ((RB, CB), F32),
        ((4, RB, LANE), F32),
        ((8, CB), F32),
        ((6, RB, 2 * LANE), BF16),
        ((NCOL, 32, LANE), F32),
    ]
    scratch = [
        ((CB, LANE), F32),
        ((RB, LANE), F32),
        ((RB, LANE), F32),
        ((6, 96, CB), BF16),
        ((NCOL, 8, CB), F32),
    ]
    return call(build_kernel, outs, scratch, 400_000_000, 8)(gotv, gotm)


def run_first_own(got, v):
    return call(first_own_kernel, [((NCOL, 32, LANE), F32)], [], 100_000, 4)(got, v)[0]


def run_second(got, t):
    scratch = [((RB, LANE), F32), ((6, 96, RB), BF16), ((48, CB), F32)]
    return call(second_kernel, [((NROW, 24, LANE), F32)], scratch, 200_000_000, 6)(got, t)[0]


def run_second_own(got, seeds, pol):
    outs = [((48, BEAD), F32), ((NROW, 24, LANE), F32)]
    return call(second_own_kernel, outs, [], 100_000, 4)(got, seeds, pol)


def run_gradient(got, l, xb, f5, g7, xc):
    outs = [((NCOL, 8, LANE), F32), ((NROW, 8, LANE), F32)]
    scratch = [
        ((CB, LANE), F32),
        ((CB, 2 * LANE), BF16),
        ((6, RB, 256), F32),
        ((3, RB, LANE), F32),
        ((8, CB), F32),
    ]
    return call(gradient_kernel, outs, scratch, 300_000_000, 12)(got, l, xb, f5, g7, xc)


def run_final(rgot, cgot):
    return call(final_kernel, [((3, BEAD), F32)], [], 100_000, 4)(rgot, cgot)[0]


def exchange(x, axis):
    return lax.all_to_all(x, axis, 0, 0, tiled=True)


def local(positions, polarizability, seeds, dipoles, tile_mask):
    seeds = seeds.reshape(48, BEAD)
    pol = polarizability[None, :]
    placed = ((seeds, 0), (dipoles.reshape(48, BEAD), 48), (positions, 96), (pol, 99))
    placed += ((tile_mask.astype(F32), 104),)
    own_v, all_mu = run_prep(
        sum(jnp.pad(x, ((at, 112 - at - x.shape[0]), (0, BEAD - x.shape[1]))) for x, at in placed)
    )
    got_mu = exchange(all_mu, ROWS_OVER)
    got_v = exchange(run_relay(got_mu, own_v), COLS_OVER)
    t, f5, g7, xb, xc, moments, parts = run_build(got_v, got_mu)
    own_next = run_first_own(exchange(parts, ROWS_OVER), own_v)
    pieces = run_second(exchange(own_next, ROWS_OVER), t)
    field, own_adjoint = run_second_own(exchange(pieces, COLS_OVER), seeds, pol)
    out_r, out_c = run_gradient(exchange(own_adjoint, COLS_OVER), moments, xb, f5, g7, xc)
    gradient = run_final(exchange(out_r, ROWS_OVER), exchange(out_c, COLS_OVER))
    return (field.reshape(3, 16, BEAD), gradient)


def solution(mesh):
    named = Mesh(mesh.devices.reshape(SIZES), AXES)
    in_specs = (P(None, AXES), P(AXES), P(None, None, AXES), P(None, None, AXES), P(AXES[:3], AXES[3:]))
    out_specs = (P(None, None, AXES), P(None, AXES))
    return jax.shard_map(local, mesh=named, in_specs=in_specs, out_specs=out_specs, check_vma=False)
```
